32 devices in a mesh: dp: 4 (over z), row: 4 (over x, core), col: 2 (over y).
Axes of the slice: x: 2, y: 2, z: 4, core: 2. Of those that a mesh axis runs over, the one named last changes fastest.
Arguments:
- block_input: bfloat16 [4096, 2560], P('dp', ('row', 'col')), may hold values from -30 to 30
- first_gain: float32 [2560], P(('row', 'col')), may hold values from 0.5 to 1.5
- query_weight: bfloat16 [2560, 2560], P('row', 'col'), may hold values from -0.125 to 0.125
- key_weight: bfloat16 [2560, 256], P('row'), may hold values from -0.125 to 0.125
- value_weight: bfloat16 [2560, 256], P('row'), may hold values from -0.125 to 0.125
- output_weight: bfloat16 [2560, 2560], P('col', 'row'), may hold values from -0.625 to 0.625
- second_gain: float32 [2560], P(('row', 'col')), may hold values from 0.5 to 1.5
- gate_weight: bfloat16 [2560, 7680], P('row', 'col'), may hold values from -0.125 to 0.125
- up_weight: bfloat16 [2560, 7680], P('row', 'col'), may hold values from -0.125 to 0.125
- down_weight: bfloat16 [7680, 2560], P('col', 'row'), may hold values from -0.0625 to 0.0625
- cotangent: bfloat16 [4096, 2560], P('dp', ('row', 'col')), may hold values from -6 to 6
- segment_ids: int32 [4, 1024], P('dp'), may hold values from 0 to 5, never falling along the last dimension, each value on 1 to 512 neighbouring positions
Outputs:
- block_output: bfloat16 [4096, 2560], P('dp', ('row', 'col'))
- input_grad: float32 [4096, 2560], P('dp', ('row', 'col'))
- first_gain_grad: float32 [2560], P(('row', 'col', 'dp'))
- query_weight_grad: float32 [2560, 2560], P(('row', 'dp'), 'col')
- key_weight_grad: float32 [2560, 256], P(('row', 'dp'))
- value_weight_grad: float32 [2560, 256], P(('row', 'dp'))
- output_weight_grad: float32 [2560, 2560], P(('col', 'dp'), 'row')
- second_gain_grad: float32 [2560], P(('row', 'col', 'dp'))
- gate_weight_grad: float32 [2560, 7680], P(('row', 'dp'), 'col')
- up_weight_grad: float32 [2560, 7680], P(('row', 'dp'), 'col')
- down_weight_grad: float32 [7680, 2560], P(('col', 'dp'), 'row')
The draws below stay inside these ranges and needn't reach their ends.
Inputs may be any that keep to these rules, and one draw needn't show every extreme that they name: `segment_ids`: along each sequence the ids never fall; each document holds 1 to 512 tokens and one holds exactly that many.
All inputs are finite; a program needn't handle non-finite values.
Results may differ from the reference program's by a relative error of at most 0.015.
The reference program's roundings to bfloat16 on the way count: a program that leaves them out, or rounds other values in their place, can miss the bound.
Values may be sent and summed in bfloat16 or wider, within the bound.
No kernel may reach another device: no remote copies, remote signals or barrier semaphores. Data moves between devices by JAX's collectives and lax.ppermute only.
A program may use at most 256 MiB of HBM per device.

```python
import math
import jax
import jax.numpy as jnp
import numpy as np
from jax import lax

D = 2560
HEADS = 10
HD = 256
FF = 7680
DOCS = 6
SEQ_LEN = 1024
SEQS = 4
TOKENS = 4096


def draw_block_input(key, part):
    column = jnp.arange(D, dtype=jnp.float32) / D
    column_scale = jnp.exp(math.log(3.0) * (column - 0.5) + jax.random.uniform(jax.random.fold_in(key, 1), (D,), jnp.float32, -0.7, 0.7))
    row_scale = jnp.exp(jax.random.uniform(jax.random.fold_in(key, 2), (TOKENS, 1), jnp.float32, -1.15, 1.15))
    noise = jnp.clip(jax.random.normal(jax.random.fold_in(key, 3), (TOKENS, D), jnp.float32), -4.0, 4.0)
    return jnp.clip(noise * row_scale * column_scale[None, :], -30.0, 30.0).astype(jnp.bfloat16)


def shard_levels(rng, dims, shards, least, high):
    level, own = 1.0, jax.random.fold_in(rng, 6)
    for axis_at, shards_of in shards:
        draws = jnp.exp(jax.random.uniform(jax.random.fold_in(own, axis_at), (shards_of,), jnp.float32, least / len(shards), high / len(shards)))
        level = level * jnp.repeat(draws, dims[axis_at] // shards_of).reshape([-1 if axis == axis_at else 1 for axis in range(len(dims))])
    return level


def profile(count, total, limit, slope):
    loads = [(1 << 20) // math.isqrt(grade ** slope) + 1 for grade in range(2, count + 1)]
    surplus, counts = total - limit - (count - 1), [1] * (count - 1)
    while surplus > 0:
        candidates = [i for i in range(count - 1) if counts[i] < limit]
        whole, budget = sum([loads[i] for i in candidates]), surplus
        for i in candidates:
            addition = min(limit - counts[i], max(1, budget * loads[i] // whole), surplus)
            counts[i] = counts[i] + addition
            surplus = surplus - addition
    return np.array([limit] + counts)


def ragged(own_key, number_of, total, limit, lean):
    if number_of == 2:
        one = jax.random.randint(own_key, (), max(1, total - limit), min(limit, total - 1) + 1)
        return jnp.stack([one, total - one])
    sizes = jnp.asarray(profile(number_of, total, limit, lean), jnp.int32)
    couples = (number_of - 1) // 2
    source_of, sink = sizes[1:1 + 2 * couples:2], sizes[2:2 + 2 * couples:2]
    slack = jnp.minimum(source_of - 1, limit - sink)
    passed = jax.random.randint(jax.random.fold_in(own_key, 1), (couples,), 0, 1 << 20) % (slack + 1)
    sizes = sizes.at[1:1 + 2 * couples:2].set(source_of - passed).at[2:2 + 2 * couples:2].set(sink + passed)
    return sizes[jax.random.permutation(jax.random.fold_in(own_key, 2), number_of)]


def scatter_about(rng, shape, deviation, reach, cuts=(), kind=jnp.bfloat16):
    entries = deviation * jax.random.normal(rng, shape, jnp.float32)
    if cuts:
        entries = entries * shard_levels(rng, shape, cuts, -0.22, 0.18)
    return jnp.clip(entries, -reach, reach).astype(kind)


def setup_inputs(seed: int = 0) -> dict:
    key_list = jax.random.split(jax.random.key(seed), 13)
    return {
        "block_input": draw_block_input(jax.random.fold_in(key_list[12], 71), 0),
        "first_gain": jnp.clip(1.0 + 0.1 * jax.random.normal(key_list[1], (D,), jnp.float32), 0.5, 1.5),
        "query_weight": scatter_about(key_list[2], (D, HEADS * HD), D ** -0.5, 0.125, ((0, 4), (1, 2))),
        "key_weight": scatter_about(key_list[3], (D, HD), D ** -0.5, 0.125, ((0, 4),)),
        "value_weight": scatter_about(key_list[4], (D, HD), D ** -0.5, 0.125, ((0, 4),)),
        "output_weight": scatter_about(key_list[5], (HEADS * HD, D), (HEADS * HD // 32) ** -0.5, 0.625, ((0, 2), (1, 4))),
        "second_gain": jnp.clip(1.0 + 0.1 * jax.random.normal(key_list[6], (D,), jnp.float32), 0.5, 1.5),
        "gate_weight": scatter_about(key_list[7], (D, FF), D ** -0.5, 0.125, ((0, 4), (1, 2))),
        "up_weight": scatter_about(key_list[8], (D, FF), D ** -0.5, 0.125, ((0, 4), (1, 2))),
        "down_weight": scatter_about(key_list[9], (FF, D), FF ** -0.5, 0.0625, ((0, 2), (1, 4))),
        "cotangent": scatter_about(key_list[10], (TOKENS, D), 1.0, 6.0, ((0, 4), (1, 8))),
        "segment_ids": jax.vmap(lambda own: jnp.searchsorted(jnp.cumsum(ragged(own, DOCS, SEQ_LEN, SEQ_LEN // 2, 1)), jnp.arange(SEQ_LEN), side="right"))(jax.random.split(key_list[11], SEQS)).reshape((SEQS, SEQ_LEN)).astype(jnp.int32),
    }


EPSILON = 1e-06
NEGATIVE = -1e+30

def matmul(left, right):
    return jnp.dot(left, right, preferred_element_type=jnp.float32)

def times_transposed(left, right):
    return lax.dot_general(left, right, (((1,), (1,)), ((), ())), preferred_element_type=jnp.float32)

def transposed_times(left, right):
    return lax.dot_general(left, right, (((0,), (0,)), ((), ())), preferred_element_type=jnp.float32)

def gelu_tanh(value):
    return jax.nn.gelu(value, approximate=True)

def rotary_tables(positions, quarter):
    freqs = jnp.exp(-jnp.log(10000.0) * jnp.arange(quarter, dtype=jnp.float32) / quarter)
    angles = positions.astype(jnp.float32)[:, None] * freqs[None, :]
    return (jnp.cos(angles), jnp.sin(angles))

def rotate(field, cosine, sine, sign):
    quarter = cosine.shape[-1]
    first = field[..., :quarter]
    second = field[..., quarter:2 * quarter]
    return jnp.concatenate([first * cosine - sign * second * sine, second * cosine + sign * first * sine, field[..., 2 * quarter:]], axis=-1)

def token_positions(segment_row):
    length = segment_row.shape[0]
    index = jnp.arange(length, dtype=jnp.int32)
    starts = jnp.concatenate([jnp.ones((1,), jnp.int32), (segment_row[1:] != segment_row[:-1]).astype(jnp.int32)])
    first = lax.cummax(jnp.where(starts > 0, index, 0), axis=0)
    return index - first

def norm_forward(values, gain):
    inverse = lax.rsqrt(lax.optimization_barrier(jnp.mean(values * values, axis=1, keepdims=True)) + EPSILON)
    normed = values * inverse
    return (normed, inverse, (normed * gain).astype(jnp.bfloat16))

def norm_backward(grad, normed, inverse, gain):
    scaled = grad * gain
    return (inverse * (scaled - normed * lax.optimization_barrier(jnp.mean(scaled * normed, axis=1, keepdims=True))), lax.optimization_barrier(jnp.sum(grad * normed, axis=0)))

def one_sequence(params, block_row, cot_row, segment_row):
    first_gain, query_weight, key_weight, value_weight, output_weight, second_gain, gate_weight, up_weight, down_weight = params
    length = block_row.shape[0]
    index = jnp.arange(length, dtype=jnp.int32)
    cosine, sine = rotary_tables(token_positions(segment_row), HD // 4)
    head_cos = cosine[:, None, :]
    head_sin = sine[:, None, :]
    scale = 1.0 / math.sqrt(HD)
    inputs = block_row.astype(jnp.float32)
    normed_one, inverse_one, wide_one = norm_forward(inputs, first_gain)
    query = rotate(matmul(wide_one, query_weight).reshape(length, HEADS, HD), head_cos, head_sin, 1.0).astype(jnp.bfloat16)
    keys = rotate(matmul(wide_one, key_weight), cosine, sine, 1.0).astype(jnp.bfloat16)
    values = matmul(wide_one, value_weight).astype(jnp.bfloat16)
    allowed = (segment_row[:, None] == segment_row[None, :]) & (index[None, :] <= index[:, None])
    scores = jnp.einsum('qhd,kd->hqk', query.astype(jnp.float32), keys.astype(jnp.float32)) * scale
    scores = jnp.where(allowed[None], scores, NEGATIVE)
    peak = lax.optimization_barrier(jnp.max(scores, axis=2, keepdims=True))
    logsum = peak + jnp.log(lax.optimization_barrier(jnp.sum(jnp.exp(scores - peak), axis=2, keepdims=True)))
    weights = jnp.exp(scores - logsum)
    probs = weights.astype(jnp.bfloat16)
    attended = jnp.einsum('hqk,kd->qhd', probs.astype(jnp.float32), values.astype(jnp.float32)).astype(jnp.bfloat16)
    attended = attended.reshape(length, HEADS * HD)
    residual = inputs + matmul(attended, output_weight)
    normed_two, inverse_two, wide_two = norm_forward(residual, second_gain)
    gate = matmul(wide_two, gate_weight)
    up = matmul(wide_two, up_weight)
    activation, gelu_back = jax.vjp(gelu_tanh, gate)
    hidden = (activation * up).astype(jnp.bfloat16)
    block_output = (residual + matmul(hidden, down_weight)).astype(jnp.bfloat16)
    down_weight_grad = transposed_times(hidden, cot_row)
    hidden_grad = times_transposed(cot_row, down_weight)
    gate_grad = gelu_back(hidden_grad * up)[0].astype(jnp.bfloat16)
    up_grad = (hidden_grad * activation).astype(jnp.bfloat16)
    gate_weight_grad = transposed_times(wide_two, gate_grad)
    up_weight_grad = transposed_times(wide_two, up_grad)
    wide_two_grad = times_transposed(gate_grad, gate_weight) + times_transposed(up_grad, up_weight)
    residual_norm, second_gain_grad = norm_backward(wide_two_grad, normed_two, inverse_two, second_gain)
    residual_grad = cot_row.astype(jnp.float32) + residual_norm
    residual_back = residual_grad.astype(jnp.bfloat16)
    output_weight_grad = transposed_times(attended, residual_back)
    attended_grad = times_transposed(residual_back, output_weight).astype(jnp.bfloat16).reshape(length, HEADS, HD)
    grad_float = attended_grad.astype(jnp.float32)
    value_grad = jnp.einsum('hqk,qhd->kd', probs.astype(jnp.float32), grad_float)
    prob_grad = jnp.einsum('qhd,kd->hqk', grad_float, values.astype(jnp.float32))
    delta = jnp.einsum('qhd,qhd->hq', grad_float, attended.reshape(length, HEADS, HD).astype(jnp.float32))[:, :, None]
    score_grad = (weights * (prob_grad - delta)).astype(jnp.bfloat16).astype(jnp.float32)
    query_grad = rotate(jnp.einsum('hqk,kd->qhd', score_grad, keys.astype(jnp.float32)) * scale, head_cos, head_sin, -1.0)
    query_grad = query_grad.astype(jnp.bfloat16).reshape(length, HEADS * HD)
    key_grad = rotate(jnp.einsum('hqk,qhd->kd', score_grad, query.astype(jnp.float32)) * scale, cosine, sine, -1.0).astype(jnp.bfloat16)
    value_back = value_grad.astype(jnp.bfloat16)
    query_weight_grad = transposed_times(wide_one, query_grad)
    key_weight_grad = transposed_times(wide_one, key_grad)
    value_weight_grad = transposed_times(wide_one, value_back)
    wide_one_grad = times_transposed(query_grad, query_weight) + times_transposed(key_grad, key_weight) + times_transposed(value_back, value_weight)
    input_norm, first_gain_grad = norm_backward(wide_one_grad, normed_one, inverse_one, first_gain)
    input_grad = residual_grad + input_norm
    grads = (first_gain_grad, query_weight_grad, key_weight_grad, value_weight_grad, output_weight_grad, second_gain_grad, gate_weight_grad, up_weight_grad, down_weight_grad)
    return (block_output, input_grad, grads)

def reference(block_input, first_gain, query_weight, key_weight, value_weight, output_weight, second_gain, gate_weight, up_weight, down_weight, cotangent, segment_ids):
    count = segment_ids.shape[0]
    length = segment_ids.shape[1]
    params = (first_gain, query_weight, key_weight, value_weight, output_weight, second_gain, gate_weight, up_weight, down_weight)

    def step(carry, items):
        block_row, cot_row, segment_row = items
        output_row, grad_row, grads = one_sequence(params, block_row, cot_row, segment_row)
        return (tuple((total + grad for total, grad in zip(carry, grads))), (output_row, grad_row))
    initial = tuple((jnp.zeros(param.shape, jnp.float32) for param in params))
    totals, (outputs, input_grads) = lax.scan(step, initial, (block_input.reshape(count, length, D), cotangent.reshape(count, length, D), segment_ids))
    return (outputs.reshape(count * length, D), input_grads.reshape(count * length, D), totals[0], totals[1], totals[2], totals[3], totals[4], totals[5], totals[6], totals[7], totals[8])
```

```python
import math

import jax
import jax.numpy as jnp
from jax import lax
from jax.sharding import PartitionSpec as P

D = 2560
HD = 256
DOCS = 6


EPSILON = 1e-06
NEGATIVE = -1e30

ROWS = 4
COLS = 2

BF = jnp.bfloat16
F32 = jnp.float32


def matmul(left, right):
    return jnp.dot(left, right, preferred_element_type=F32)


def times_transposed(left, right):
    return lax.dot_general(left, right, (((1,), (1,)), ((), ())), preferred_element_type=F32)


def transposed_times(left, right):
    return lax.dot_general(left, right, (((0,), (0,)), ((), ())), preferred_element_type=F32)


def gelu_tanh(value):
    return jax.nn.gelu(value, approximate=True)


def swap(value, axis, distance):
    size = lax.axis_size(axis)
    return lax.ppermute(value, axis, [(i, i ^ distance) for i in range(size)])


def over_row(value, distance):
    return swap(value, "row", distance)


def over_col(value):
    return swap(value, "col", 1)


def after(value, *others):
    return lax.optimization_barrier((value, *others))[0]


def rotary_tables(positions, quarter):
    freqs = jnp.exp(-jnp.log(10000.0) * jnp.arange(quarter, dtype=F32) / quarter)
    angles = positions.astype(F32)[:, None] * freqs[None, :]
    return (jnp.cos(angles), jnp.sin(angles))


def rotate(field, cosine, sine, sign):
    quarter = cosine.shape[-1]
    first = field[..., :quarter]
    second = field[..., quarter : 2 * quarter]
    return jnp.concatenate(
        [
            first * cosine - sign * second * sine,
            second * cosine + sign * first * sine,
            field[..., 2 * quarter :],
        ],
        axis=-1,
    )


def token_layout(segment_ids):
    count, length = segment_ids.shape
    index = jnp.arange(length, dtype=jnp.int32)[None, :]
    starts = jnp.concatenate(
        [
            jnp.ones((count, 1), jnp.int32),
            (segment_ids[:, 1:] != segment_ids[:, :-1]).astype(jnp.int32),
        ],
        axis=1,
    )
    first = lax.cummax(jnp.where(starts > 0, index, 0), axis=1)
    positions = (index - first).reshape(-1)
    documents = (segment_ids + DOCS * jnp.arange(count, dtype=jnp.int32)[:, None]).reshape(-1)
    return (positions, documents)


def masked_scores(rows, keys, query_docs, query_index, key_docs, key_index):
    scores = jnp.einsum("qhd,kd->hqk", rows, keys, preferred_element_type=F32) * (
        1.0 / math.sqrt(keys.shape[1])
    )
    allowed = (query_docs[:, None] == key_docs[None, :]) & (
        key_index[None, :] <= query_index[:, None]
    )
    return jnp.where(allowed[None], scores, NEGATIVE)


def attention_forward(query, keys, values, layout):
    scores = masked_scores(query, keys, *layout)
    peak = jnp.max(scores, axis=2, keepdims=True)
    logsum = peak + jnp.log(jnp.sum(jnp.exp(scores - peak), axis=2, keepdims=True))
    probs = jnp.exp(scores - logsum).astype(BF)
    output = jnp.einsum("hqk,kd->qhd", probs, values, preferred_element_type=F32).astype(BF)
    return (output.reshape(query.shape[0], -1), logsum)


def attention_backward(query, keys, values, attended, attended_grad, logsum, layout):
    scale = 1.0 / math.sqrt(query.shape[2])
    outputs = attended.reshape(query.shape)
    scores = masked_scores(query, keys, *layout)
    weights = jnp.exp(scores - logsum)
    value_grad = jnp.einsum(
        "hqk,qhd->kd", weights.astype(BF), attended_grad, preferred_element_type=F32
    )
    prob_grad = jnp.einsum("qhd,kd->hqk", attended_grad, values, preferred_element_type=F32)
    delta = jnp.einsum("qhd,qhd->hq", attended_grad, outputs, preferred_element_type=F32)
    score_grad = (weights * (prob_grad - delta[:, :, None])).astype(BF)
    query_grad = jnp.einsum("hqk,kd->qhd", score_grad, keys, preferred_element_type=F32) * scale
    key_grad = jnp.einsum("hqk,qhd->kd", score_grad, query, preferred_element_type=F32) * scale
    return (key_grad, value_grad, query_grad)


def on_device(
    block_input,
    first_gain,
    query_weight,
    key_weight,
    value_weight,
    output_weight,
    second_gain,
    gate_weight,
    up_weight,
    down_weight,
    cotangent,
    segment_ids,
):
    row = lax.axis_index("row")
    col = lax.axis_index("col")
    depth = lax.axis_index("dp")
    depths = lax.axis_size("dp")
    assert lax.axis_size("row") == ROWS and lax.axis_size("col") == COLS
    tokens, width = block_input.shape
    wide_width = COLS * width
    span = tokens // ROWS
    part = span // COLS
    query_width = query_weight.shape[1]
    heads = query_width // HD
    ff_width = gate_weight.shape[1]
    ff = ff_width // ROWS

    def exchange_rows(blocks):
        low, high = (row & 1) == 1, (row >> 1) == 1
        picked = [
            jnp.where(
                high,
                jnp.where(low, blocks[j ^ 3], blocks[j ^ 2]),
                jnp.where(low, blocks[j ^ 1], blocks[j]),
            )
            for j in range(ROWS)
        ]
        return picked

    def block_of(value, jr, jy):
        return lax.dynamic_slice_in_dim(value, ((row ^ jr) * COLS + (col ^ jy)) * part, part, 0)

    def reorder(value):
        return jnp.concatenate(
            [block_of(value, jr, jy) for jr in range(ROWS) for jy in range(COLS)], axis=0
        )

    def reorder_col_major(value):
        return jnp.concatenate(
            [block_of(value, jr, jy) for jy in range(COLS) for jr in range(ROWS)], axis=0
        )

    def pair_cols(own, other):
        return jnp.concatenate([jnp.where(col == 0, own, other), jnp.where(col == 0, other, own)], axis=1)

    def own_cols(value):
        return jnp.where(col == 0, value[..., :width], value[..., width:])

    def other_cols(value):
        return jnp.where(col == 0, value[..., width:], value[..., :width])

    def plane_sum(value):
        shape = value.shape
        value = value.reshape(8, -1)
        value = value + over_row(value, 1)
        value = value + over_row(value, 2)
        value = value + over_col(value)
        return value.reshape(shape)

    def wide_weights(value):
        n = value.shape[1] // ROWS
        return [value[:, k * n : (k + 1) * n] for k in range(ROWS)]

    input_other = over_col(block_input)
    own_float = block_input.astype(F32)
    squares = plane_sum(jnp.sum(own_float * own_float, axis=1))
    inverse_natural = lax.rsqrt(squares / D + EPSILON)
    gains = jnp.stack([first_gain, second_gain])
    gains = pair_cols(gains, over_col(gains))
    second_blocks = [gains[1]] + [over_row(gains[1], k) for k in range(1, ROWS)]
    second_wide = jnp.concatenate(exchange_rows(second_blocks))

    rows_per_depth = wide_width // depths
    gate_blocks = wide_weights(gate_weight)
    up_blocks = wide_weights(up_weight)
    both_blocks = exchange_rows([jnp.concatenate([a, b], axis=1) for a, b in zip(gate_blocks, up_blocks)])
    start = depth * rows_per_depth
    far = [
        over_row(lax.dynamic_slice_in_dim(both_blocks[k], start, rows_per_depth, 0), k) for k in (2, 3)
    ]
    near = over_row(both_blocks[1], 1)
    far = lax.all_gather(jnp.stack(far), "dp", axis=1, tiled=True)
    both_rows = exchange_rows([both_blocks[0], near, far[0], far[1]])
    gate_wide = jnp.concatenate([b[:, :ff] for b in both_rows], axis=0)
    up_wide = jnp.concatenate([b[:, ff:] for b in both_rows], axis=0)

    input_wide = reorder(pair_cols(block_input, input_other))
    inverse_one = reorder(inverse_natural)[:, None]
    wide_one = (input_wide.astype(F32) * inverse_one * gains[0]).astype(BF)
    input_blocks = input_wide.reshape(ROWS, COLS, part, wide_width)

    def to_token_shard(blocks):
        received = [blocks[0]] + [over_row(blocks[k], k) for k in range(1, ROWS)]
        return jnp.concatenate(exchange_rows(received), axis=1)

    positions, documents = token_layout(segment_ids)
    positions = reorder(positions)
    documents = reorder(documents)
    key_index = reorder(jnp.arange(tokens, dtype=jnp.int32))
    cosine, sine = rotary_tables(positions, HD // 4)
    query_cos = cosine[:span, None, :]
    query_sin = sine[:span, None, :]
    layout = (documents[:span], key_index[:span], documents, key_index)

    def row_block(value, j):
        return value[j * span : (j + 1) * span]

    def pair_rows(value, a, b):
        return jnp.concatenate([row_block(value, a), row_block(value, b)], axis=0)

    def row_scatter(product, value):
        sent = over_row(product(pair_rows(value, 1, 3)).astype(BF), 1)
        kept = product(pair_rows(value, 0, 2)) + sent.astype(F32)
        sent = over_row(kept[span:].astype(BF), 2)
        return kept[:span] + sent.astype(F32)

    def row_gather(value):
        near_block = over_row(value, 1)
        far_block = over_row(value, 2)
        return [value, near_block, far_block, over_row(far_block, 1)]

    kv_weight = jnp.concatenate([key_weight, value_weight], axis=1)
    kv_sent = over_row(matmul(pair_rows(wide_one, 1, 3), kv_weight).astype(BF), 1)
    query_raw = row_scatter(lambda part_value: matmul(part_value, query_weight), wide_one)
    kv_kept = matmul(pair_rows(wide_one, 0, 2), kv_weight) + kv_sent.astype(F32)
    kv_other = over_row(kv_kept.astype(BF), 2)
    kv_raw = kv_kept + jnp.concatenate([kv_other[span:], kv_other[:span]], axis=0).astype(F32)
    query = rotate(query_raw.reshape(span, heads, HD), query_cos, query_sin, 1.0).astype(BF)
    pair_cos, pair_sin = pair_rows(cosine, 0, 2), pair_rows(sine, 0, 2)
    kv_pair = jnp.concatenate(
        [rotate(kv_raw[:, :HD], pair_cos, pair_sin, 1.0), kv_raw[:, HD:]], axis=1
    ).astype(BF)

    def unpair(own, other):
        return jnp.concatenate([own[:span], other[:span], own[span:], other[span:]], axis=0)

    kv_all = unpair(kv_pair, over_row(kv_pair, 1))
    keys, values = kv_all[:, :HD], kv_all[:, HD:]

    attended, logsum = attention_forward(query, keys, values, layout)
    attended_blocks = row_gather(attended)

    def project(blocks):
        return matmul(jnp.concatenate(blocks, axis=0), output_weight).reshape(
            2, COLS, part, wide_width
        )

    near_out = project(attended_blocks[:2])
    far_out = project(attended_blocks[2:])
    out_sent = over_col(jnp.stack([near_out[:, 1], far_out[:, 1]]).astype(BF))
    out_sum = jnp.stack([near_out[:, 0], far_out[:, 0]]) + out_sent.astype(F32)
    out_sum = out_sum.reshape(ROWS, part, wide_width)
    out_rounded = out_sum.astype(BF)
    residual = (
        to_token_shard([input_blocks[k, 0] for k in range(ROWS)]).astype(F32)
        + to_token_shard([out_rounded[k] for k in range(ROWS)]).astype(F32)
    )

    inverse_two = lax.rsqrt(jnp.sum(residual * residual, axis=1, keepdims=True) / D + EPSILON)
    normed_two = residual * inverse_two
    own = (normed_two * second_wide).astype(BF)
    half = part // 2
    at_x, at_y = over_row(own, 2), over_col(own)
    at_c = over_row(own, 1)
    at_xc, at_yc = over_row(at_x, 1), over_row(at_y, 1)
    at_xy = jnp.concatenate([over_row(at_y[:half], 2), over_col(at_x[half:])], axis=0)
    at_xyc = over_row(at_xy, 1)
    groups = ([own, at_c], [at_x, at_xc, at_y, at_yc], [at_xy, at_xyc])

    cot_wide = pair_cols(cotangent, over_col(cotangent))
    down_blocks = [
        lax.dynamic_slice_in_dim(down_weight, (row ^ j) * ff, ff, 0) for j in range(ROWS)
    ]

    def hidden_part(j):
        return times_transposed(cot_wide, down_blocks[j])

    far_kept = hidden_part(2) + over_row(hidden_part(3).astype(BF), 1).astype(F32)
    near_kept = hidden_part(0) + over_row(hidden_part(1).astype(BF), 1).astype(F32)
    hidden_grad = near_kept + over_row(far_kept.astype(BF), 2).astype(F32)
    hidden_grad = reorder_col_major(hidden_grad)

    sizes = [len(g) * part for g in groups]
    offset = 0
    hiddens, gate_grads, up_grads, wides = [], [], [], []
    for group, size in zip(groups, sizes):
        wide = jnp.concatenate(group, axis=0)
        gate = matmul(wide, gate_wide)
        up = matmul(wide, up_wide)
        grad = hidden_grad[offset : offset + size]
        offset += size
        activation, gelu_back = jax.vjp(gelu_tanh, gate)
        hiddens.append((activation * up).astype(BF))
        gate_grads.append(gelu_back(grad * up)[0].astype(BF))
        up_grads.append((grad * activation).astype(BF))
        wides.append(wide)
    wide_two = jnp.concatenate(wides, axis=0)
    hidden = jnp.concatenate(hiddens, axis=0)
    gate_grad = jnp.concatenate(gate_grads, axis=0)
    up_grad = jnp.concatenate(up_grads, axis=0)

    def over_depth(value):
        return lax.psum_scatter(value, "dp", scatter_dimension=0, tiled=True)

    feed = jnp.stack(
        [transposed_times(wide_two, gate_grad).astype(BF), transposed_times(wide_two, up_grad).astype(BF)]
    ).reshape(2, ROWS, depths, rows_per_depth, ff)
    feed = feed.transpose(2, 0, 1, 3, 4).reshape(depths * 2 * ROWS * rows_per_depth, ff)
    feed = over_depth(feed).reshape(2, ROWS, rows_per_depth, ff)
    feed_blocks = exchange_rows([feed[:, k] for k in range(ROWS)])
    feed_blocks = [feed_blocks[0]] + [over_row(feed_blocks[k], k) for k in range(1, ROWS)]
    feed = jnp.concatenate(exchange_rows(feed_blocks), axis=2).astype(F32)

    def picks(value, blocks):
        return jnp.concatenate([value[b * part : (b + 1) * part] for b in blocks], axis=0)

    def plane_product(blocks):
        return times_transposed(picks(gate_grad, blocks), gate_wide) + times_transposed(
            picks(up_grad, blocks), up_wide
        )

    sent = over_row(plane_product((1, 3, 5, 7)).astype(BF), 1)
    kept = plane_product((0, 2, 4, 6)) + sent.astype(F32)
    kept = kept.reshape(2, 2, part, D)
    left, right = kept[..., : D // 2], kept[..., D // 2 :]
    left = left[0] + over_col(left[1].astype(BF)).astype(F32)
    left = left[0] + over_row(left[1].astype(BF), 2).astype(F32)
    right = right[:, 0] + over_row(right[:, 1].astype(BF), 2).astype(F32)
    right = right[0] + over_col(right[1].astype(BF)).astype(F32)
    wide_two_grad = jnp.concatenate([left, right], axis=1)

    cot_rel = reorder(cot_wide).reshape(ROWS, COLS, part, wide_width)
    cot_shard = to_token_shard([cot_rel[k, 0] for k in range(ROWS)]).astype(F32)
    scaled = wide_two_grad * second_wide
    inner = jnp.sum(scaled * normed_two, axis=1, keepdims=True)
    residual_grad = cot_shard + inverse_two * (scaled - normed_two * (inner / D))
    second_partial = jnp.sum(wide_two_grad * normed_two, axis=0)
    residual_back = residual_grad.astype(BF)

    residual_other = over_col(residual_back)
    residual_cols = jnp.concatenate([residual_back, residual_other], axis=0)
    column_blocks = exchange_rows(
        [residual_cols[:, k * wide_width : (k + 1) * wide_width] for k in range(ROWS)]
    )
    residual_blocks = [column_blocks[0]] + [over_row(column_blocks[k], k) for k in range(1, ROWS)]
    residual_wide = jnp.concatenate(residual_blocks, axis=0)

    attended_grad = row_scatter(
        lambda part_value: times_transposed(part_value, output_weight), residual_wide
    ).astype(BF)
    key_grad, value_grad, query_grad = attention_backward(
        query, keys, values, attended, attended_grad.reshape(span, heads, HD), logsum, layout
    )
    query_grad = (
        rotate(query_grad, query_cos, query_sin, -1.0).reshape(span, query_width).astype(BF)
    )
    query_grad_all = jnp.concatenate(row_gather(query_grad), axis=0)
    kv_grad = jnp.concatenate([key_grad, value_grad], axis=1)
    kv_pair_grad = pair_rows(kv_grad, 0, 2) + over_row(pair_rows(kv_grad, 1, 3).astype(BF), 1).astype(
        F32
    )
    def flip_cols(value):
        shape = value.shape
        value = value.reshape(-1, COLS, part, shape[-1])
        return jnp.concatenate([value[:, 1:], value[:, :1]], axis=1).reshape(shape)

    kv_half = kv_pair_grad.astype(BF)
    kv_pair_grad = kv_half.astype(F32) + flip_cols(over_col(kv_half)).astype(F32)
    kv_half = kv_pair_grad.astype(BF)
    kv_other = over_row(kv_half, 2)
    kv_pair_grad = kv_half.astype(F32) + jnp.concatenate(
        [kv_other[span:], kv_other[:span]], axis=0
    ).astype(F32)
    kv_back_pair = jnp.concatenate(
        [rotate(kv_pair_grad[:, :HD], pair_cos, pair_sin, -1.0), kv_pair_grad[:, HD:]], axis=1
    ).astype(BF)
    kv_back = unpair(kv_back_pair, over_row(kv_back_pair, 1))

    hidden_natural = jnp.concatenate(
        [
            lax.dynamic_slice_in_dim(hidden, ((col ^ y) * ROWS + (row ^ r)) * part, part, 0)
            for r in range(ROWS)
            for y in range(COLS)
        ],
        axis=0,
    )
    hidden_natural = after(hidden_natural, residual_back)
    hidden_blocks = row_gather(hidden_natural)
    down_partial = sum(matmul(h, w) for h, w in zip(hidden_blocks, down_blocks))
    down_grad = jnp.concatenate(
        exchange_rows([transposed_times(h, cot_wide).astype(BF) for h in hidden_blocks]), axis=0
    )
    down_grad = over_depth(down_grad).astype(F32)
    mlp = own_cols(down_partial) + over_col(other_cols(down_partial).astype(BF)).astype(F32)
    out_far = over_col(other_cols(out_sum))
    out_own = jnp.stack([own_cols(out_sum), out_far], axis=1).reshape(tokens, width)
    block_output = (own_float + reorder(out_own) + mlp).astype(BF)

    attended_all = jnp.concatenate(attended_blocks, axis=0)
    output_grad = transposed_times(attended_all, residual_wide).astype(BF)
    query_weight_grad = transposed_times(wide_one, query_grad_all).astype(BF)
    kv_weight_grad = transposed_times(wide_one, kv_back).astype(BF)
    pieces = query_width // wide_width
    shared = kv_weight_grad.shape[1]
    output_rows = output_grad.shape[0] // depths
    rest = jnp.concatenate(
        [output_grad.reshape(depths, output_rows, wide_width)]
        + [
            query_weight_grad[:, k * wide_width : (k + 1) * wide_width].reshape(
                depths, rows_per_depth, wide_width
            )
            for k in range(pieces)
        ]
        + [
            jnp.pad(kv_weight_grad, ((0, 0), (0, wide_width - shared))).reshape(
                depths, rows_per_depth, wide_width
            )
        ],
        axis=1,
    )
    rest = over_depth(rest.reshape(-1, wide_width)).astype(F32)
    output_grad = rest[:output_rows]
    query_weight_grad = jnp.concatenate(
        [
            rest[output_rows + k * rows_per_depth : output_rows + (k + 1) * rows_per_depth]
            for k in range(pieces)
        ],
        axis=1,
    )
    kv_weight_grad = rest[output_rows + pieces * rows_per_depth :, :shared]

    wide_one_partial = times_transposed(query_grad_all, query_weight)
    kv_rows = jnp.where(col == 0, kv_weight[:width], kv_weight[width:])
    wide_one_grad = (
        own_cols(wide_one_partial)
        + flip_cols(over_col(other_cols(wide_one_partial).astype(BF))).astype(F32)
        + times_transposed(kv_back, kv_rows)
    )
    normed_one = own_cols(input_wide).astype(F32) * inverse_one
    scaled = wide_one_grad * first_gain
    inner = plane_sum(reorder(jnp.sum(scaled * normed_one, axis=1)))
    inner = reorder(inner)[:, None]
    input_norm = inverse_one * (scaled - normed_one * (inner / D))
    first_partial = jnp.sum(wide_one_grad * normed_one, axis=0)
    input_grad = reorder(own_cols(residual_wide).astype(F32) + input_norm)

    second_partial = second_partial.reshape(ROWS, wide_width)
    second_partial = own_cols(second_partial) + over_col(other_cols(second_partial))
    blocks = exchange_rows([second_partial[k] for k in range(ROWS)])
    blocks = jnp.stack([blocks[0], blocks[2]]) + over_row(jnp.stack([blocks[1], blocks[3]]), 1)
    second_partial = blocks[0] + over_row(blocks[1], 2)
    gain_grads = jnp.stack([first_partial, second_partial])
    distance = 1
    while distance < depths:
        gain_grads = gain_grads + swap(gain_grads, "dp", distance)
        distance *= 2
    gain_width = width // depths
    gain_grads = lax.dynamic_slice_in_dim(gain_grads, depth * gain_width, gain_width, 1)

    return (
        block_output,
        input_grad,
        gain_grads[0],
        query_weight_grad,
        kv_weight_grad[:, :HD],
        kv_weight_grad[:, HD:],
        output_grad,
        gain_grads[1],
        feed[0],
        feed[1],
        down_grad,
    )


def solution(mesh):
    return jax.shard_map(
        on_device,
        mesh=mesh,
        in_specs=(
            P("dp", ("row", "col")),
            P(("row", "col")),
            P("row", "col"),
            P("row", None),
            P("row", None),
            P("col", "row"),
            P(("row", "col")),
            P("row", "col"),
            P("row", "col"),
            P("col", "row"),
            P("dp", ("row", "col")),
            P("dp", None),
        ),
        out_specs=(
            P("dp", ("row", "col")),
            P("dp", ("row", "col")),
            P(("row", "col", "dp")),
            P(("row", "dp"), "col"),
            P(("row", "dp"), None),
            P(("row", "dp"), None),
            P(("col", "dp"), "row"),
            P(("row", "col", "dp")),
            P(("row", "dp"), "col"),
            P(("row", "dp"), "col"),
            P(("col", "dp"), "row"),
        ),
        check_vma=False,
    )
```

```python
import functools
import math

import jax
import jax.numpy as jnp
from jax import lax
from jax.experimental import pallas as pl
from jax.experimental.pallas import tpu as pltpu
from jax.sharding import PartitionSpec as P

D = 2560
HD = 256
DOCS = 6


EPSILON = 1e-06
NEGATIVE = -1e30

ROWS = 4
COLS = 2

BF = jnp.bfloat16
F32 = jnp.float32


def matmul(left, right):
    return jnp.dot(left, right, preferred_element_type=F32)


def times_transposed(left, right):
    return lax.dot_general(left, right, (((1,), (1,)), ((), ())), preferred_element_type=F32)


def transposed_times(left, right):
    return lax.dot_general(left, right, (((0,), (0,)), ((), ())), preferred_element_type=F32)


def gelu_tanh(value):
    return jax.nn.gelu(value, approximate=True)


def swap(value, axis, distance):
    size = lax.axis_size(axis)
    return lax.ppermute(value, axis, [(i, i ^ distance) for i in range(size)])


def over_row(value, distance):
    return swap(value, "row", distance)


def over_col(value):
    return swap(value, "col", 1)


def after(value, *others):
    return lax.optimization_barrier((value, *others))[0]


def rotary_tables(positions, quarter):
    freqs = jnp.exp(-jnp.log(10000.0) * jnp.arange(quarter, dtype=F32) / quarter)
    angles = positions.astype(F32)[:, None] * freqs[None, :]
    return (jnp.cos(angles), jnp.sin(angles))


def token_layout(segment_ids):
    count, length = segment_ids.shape
    index = jnp.arange(length, dtype=jnp.int32)[None, :]
    starts = jnp.concatenate(
        [
            jnp.ones((count, 1), jnp.int32),
            (segment_ids[:, 1:] != segment_ids[:, :-1]).astype(jnp.int32),
        ],
        axis=1,
    )
    first = lax.cummax(jnp.where(starts > 0, index, 0), axis=1)
    positions = (index - first).reshape(-1)
    documents = (segment_ids + DOCS * jnp.arange(count, dtype=jnp.int32)[:, None]).reshape(-1)
    return (positions, documents)


def turn(field, cosine, sine):
    first = field[:, : HD // 2]
    return jnp.concatenate(
        [first * cosine + pltpu.roll(first, HD // 4, 1) * sine, field[:, HD // 2 :]], axis=1
    )


def fill_bias(bias_ref, query_docs, query_index, key_docs, key_index):
    allowed = (query_docs[...] == key_docs[...]) & (key_index[...] <= query_index[...])
    bias_ref[...] = jnp.where(allowed, 0.0, NEGATIVE)


def forward_kernel(
    kept_ref, sent_ref, cos_ref, sin_ref, kv_ref, qd_ref, qi_ref, kd_ref, ki_ref,
    query_ref, attended_ref, logsum_ref, bias_ref,
):
    @pl.when(pl.program_id(0) == 0)
    def _():
        fill_bias(bias_ref, qd_ref, qi_ref, kd_ref, ki_ref)

    raw = kept_ref[...] + sent_ref[...].astype(F32)
    query = turn(raw, cos_ref[...], sin_ref[...]).astype(BF)
    query_ref[...] = query
    scores = times_transposed(query, kv_ref[:, :HD]) * (1.0 / math.sqrt(HD)) + bias_ref[...]
    peak = jnp.max(scores, axis=1, keepdims=True)
    weights = jnp.exp(scores - peak)
    total = jnp.sum(weights, axis=1, keepdims=True)
    logsum_ref[0] = peak + jnp.log(total)
    probs = (weights * (1.0 / total)).astype(BF)
    attended_ref[...] = matmul(probs, kv_ref[:, HD:]).astype(BF)


def attention_forward(kept, sent, tables, kv, layout):
    span, width = sent.shape
    length = kv.shape[0]
    heads = width // HD
    query_docs, query_index, key_docs, key_index = layout
    whole = lambda a: pl.BlockSpec(a.shape, lambda h: (0, 0))
    small = [
        tables[0], tables[1], kv, query_docs[:, None], query_index[:, None], key_docs[None], key_index[None]
    ]
    head = pl.BlockSpec((span, HD), lambda h: (0, h))
    return pl.pallas_call(
        forward_kernel,
        grid=(heads,),
        in_specs=[head, head] + [whole(a) for a in small],
        out_specs=[head, head, pl.BlockSpec((1, span, 1), lambda h: (h, 0, 0))],
        out_shape=[
            jax.ShapeDtypeStruct((span, width), BF),
            jax.ShapeDtypeStruct((span, width), BF),
            jax.ShapeDtypeStruct((heads, span, 1), F32),
        ],
        scratch_shapes=[pltpu.VMEM((span, length), F32)],
        name="attention_forward",
    )(kept, sent, *small)


def backward_kernel(
    query_ref, attended_ref, kept_ref, sent_ref, logsum_ref, cos_ref, sin_ref, kv_ref, qd_ref, qi_ref,
    kd_ref, ki_ref, query_grad_ref, kv_grad_ref, bias_ref,
):
    @pl.when(pl.program_id(0) == 0)
    def _():
        fill_bias(bias_ref, qd_ref, qi_ref, kd_ref, ki_ref)
        kv_grad_ref[...] = jnp.zeros_like(kv_grad_ref)

    scale = 1.0 / math.sqrt(HD)
    query = query_ref[...]
    grad = (kept_ref[...] + sent_ref[...].astype(F32)).astype(BF)
    keys, values = kv_ref[:, :HD], kv_ref[:, HD:]
    scores = times_transposed(query, keys) * scale + bias_ref[...]
    weights = jnp.exp(scores - logsum_ref[0])
    kv_grad_ref[:, HD:] += transposed_times(weights.astype(BF), grad)
    delta = jnp.sum(grad.astype(F32) * attended_ref[...].astype(F32), axis=1, keepdims=True)
    score_grad = (weights * (times_transposed(grad, values) - delta)).astype(BF)
    query_grad = turn(matmul(score_grad, keys) * scale, cos_ref[...], -sin_ref[...])
    query_grad_ref[...] = query_grad.astype(BF)
    kv_grad_ref[:, :HD] += transposed_times(score_grad, query) * scale


def attention_backward(query, attended, kept, sent, logsum, tables, kv, layout):
    span, width = sent.shape
    length = kv.shape[0]
    heads = width // HD
    query_docs, query_index, key_docs, key_index = layout
    whole = lambda a: pl.BlockSpec(a.shape, lambda h: (0, 0))
    small = [
        tables[0], tables[1], kv, query_docs[:, None], query_index[:, None], key_docs[None], key_index[None]
    ]
    head = pl.BlockSpec((span, HD), lambda h: (0, h))
    return pl.pallas_call(
        backward_kernel,
        grid=(heads,),
        in_specs=[head, head, head, head, pl.BlockSpec((1, span, 1), lambda h: (h, 0, 0))]
        + [whole(a) for a in small],
        out_specs=[head, pl.BlockSpec((length, 2 * HD), lambda h: (0, 0))],
        out_shape=[
            jax.ShapeDtypeStruct((span, width), BF),
            jax.ShapeDtypeStruct((length, 2 * HD), F32),
        ],
        scratch_shapes=[pltpu.VMEM((span, length), F32)],
        name="attention_backward",
    )(query, attended, kept, sent, logsum, *small)


def turn_kernel(kept_ref, other_ref, cos_ref, sin_ref, out_ref, *, sign):
    span = kept_ref.shape[0] // 2
    other = jnp.concatenate([other_ref[span:], other_ref[:span]], axis=0)
    total = kept_ref[...].astype(F32) + other.astype(F32)
    keys = turn(total[:, :HD], cos_ref[...], sin_ref[...] * sign)
    out_ref[...] = jnp.concatenate([keys, total[:, HD:]], axis=1).astype(BF)


def turn_pair(kept, other, cosine, sine, sign):
    return pl.pallas_call(
        functools.partial(turn_kernel, sign=sign),
        out_shape=jax.ShapeDtypeStruct(kept.shape, BF),
        name="turn_pair",
    )(kept, other, cosine, sine)


def norm_kernel(row_ref, *refs, depths):
    input_refs, out_refs = refs[:ROWS], refs[ROWS : 2 * ROWS]
    gain_ref, normed_ref, inverse_ref, wide_ref = refs[2 * ROWS :]
    row = row_ref[0]
    block = D // ROWS
    for j in range(ROWS):
        at = pl.ds(pl.multiple_of((row ^ j) * block, 128), block)
        normed_ref[:, at] = input_refs[j][...].astype(F32) + out_refs[j][...].astype(F32)
    residual = normed_ref[...]
    inverse = lax.rsqrt(jnp.sum(residual * residual, axis=1, keepdims=True) / D + EPSILON)
    normed = residual * inverse
    normed_ref[...] = normed
    inverse_ref[...] = inverse
    wide = normed * gain_ref[...]
    chunk = block // depths
    pieces = [
        wide[:, r * block + z * chunk : r * block + (z + 1) * chunk]
        for z in range(depths)
        for r in range(ROWS)
    ]
    wide_ref[...] = jnp.concatenate(pieces, axis=1).astype(BF)


def norm_shard(row, inputs, outs, gain, depths):
    part = inputs[0].shape[0]
    vmem = pl.BlockSpec(memory_space=pltpu.VMEM)
    return pl.pallas_call(
        functools.partial(norm_kernel, depths=depths),
        in_specs=[pl.BlockSpec(memory_space=pltpu.SMEM)] + [vmem] * (2 * ROWS + 1),
        out_specs=[vmem] * 3,
        out_shape=[
            jax.ShapeDtypeStruct((part, D), F32),
            jax.ShapeDtypeStruct((part, 1), F32),
            jax.ShapeDtypeStruct((part, D), BF),
        ],
        name="norm_shard",
    )(row.reshape(1), *inputs, *outs, gain[None])


def pick_kernel(where_ref, gate_ref, up_ref, *out_refs, blocks):
    width = gate_ref.shape[1] // ROWS
    for row in range(ROWS):

        @pl.when(where_ref[0] == row)
        def _(row=row):
            for block, out_ref in zip(blocks, out_refs):
                at = (row ^ block) * width
                out_ref[0] = gate_ref[:, at : at + width]
                out_ref[1] = up_ref[:, at : at + width]


def pick_columns(row, first, count, rows, gate, up, blocks):
    width = gate.shape[1] // ROWS
    source = pl.BlockSpec((rows, gate.shape[1]), lambda i, where: (where[1] + i, 0))
    return pl.pallas_call(
        functools.partial(pick_kernel, blocks=blocks),
        grid_spec=pltpu.PrefetchScalarGridSpec(
            num_scalar_prefetch=1,
            grid=(count,),
            in_specs=[source, source],
            out_specs=[pl.BlockSpec((2, rows, width), lambda i, where: (0, i, 0))] * len(blocks),
        ),
        out_shape=[jax.ShapeDtypeStruct((2, count * rows, width), BF)] * len(blocks),
        name="pick_columns",
    )(jnp.stack([row, first]), gate, up)


def assemble_kernel(row_ref, own_ref, near_ref, far_ref, gate_ref, up_ref, sems):
    copies = []
    for g, out_ref in enumerate((gate_ref, up_ref)):
        sources = (own_ref.at[g], near_ref.at[g], far_ref.at[:, 0, g], far_ref.at[:, 1, g])
        for j, source in enumerate(sources):
            copies.append(
                pltpu.make_async_copy(source, out_ref.at[:, row_ref[0] ^ j], sems.at[g * ROWS + j])
            )
    for copy in copies:
        copy.start()
    for copy in copies:
        copy.wait()


def assemble(row, own, near, far):
    depths, _, _, rows, width = far.shape
    anywhere = pl.BlockSpec(memory_space=pl.ANY)
    own = own.reshape(2, depths, rows, width)
    near = near.reshape(2, depths, rows, width)
    shape = jax.ShapeDtypeStruct((depths, ROWS, rows, width), BF)
    gate, up = pl.pallas_call(
        assemble_kernel,
        in_specs=[pl.BlockSpec(memory_space=pltpu.SMEM)] + [anywhere] * 3,
        out_specs=[anywhere] * 2,
        out_shape=[shape, shape],
        scratch_shapes=[pltpu.SemaphoreType.DMA((2 * ROWS,))],
        name="assemble",
    )(row.reshape(1), own, near, far)
    return gate.reshape(-1, width), up.reshape(-1, width)


def on_device(
    block_input,
    first_gain,
    query_weight,
    key_weight,
    value_weight,
    output_weight,
    second_gain,
    gate_weight,
    up_weight,
    down_weight,
    cotangent,
    segment_ids,
):
    row = lax.axis_index("row")
    col = lax.axis_index("col")
    depth = lax.axis_index("dp")
    depths = lax.axis_size("dp")
    assert lax.axis_size("row") == ROWS and lax.axis_size("col") == COLS
    tokens, width = block_input.shape
    wide_width = COLS * width
    span = tokens // ROWS
    part = span // COLS
    query_width = query_weight.shape[1]
    heads = query_width // HD
    ff_width = gate_weight.shape[1]
    ff = ff_width // ROWS

    def exchange_rows(blocks):
        low, high = (row & 1) == 1, (row >> 1) == 1
        picked = [
            jnp.where(
                high,
                jnp.where(low, blocks[j ^ 3], blocks[j ^ 2]),
                jnp.where(low, blocks[j ^ 1], blocks[j]),
            )
            for j in range(ROWS)
        ]
        return picked

    def block_of(value, jr, jy):
        return lax.dynamic_slice_in_dim(value, ((row ^ jr) * COLS + (col ^ jy)) * part, part, 0)

    def reorder(value):
        return jnp.concatenate(
            [block_of(value, jr, jy) for jr in range(ROWS) for jy in range(COLS)], axis=0
        )

    def reorder_col_major(value):
        return jnp.concatenate(
            [block_of(value, jr, jy) for jy in range(COLS) for jr in range(ROWS)], axis=0
        )

    def pair_cols(own, other):
        return jnp.concatenate([jnp.where(col == 0, own, other), jnp.where(col == 0, other, own)], axis=1)

    def own_cols(value):
        return jnp.where(col == 0, value[..., :width], value[..., width:])

    def other_cols(value):
        return jnp.where(col == 0, value[..., width:], value[..., :width])

    def plane_sum(value):
        shape = value.shape
        value = value.reshape(8, -1)
        value = value + over_row(value, 1)
        value = value + over_row(value, 2)
        value = value + over_col(value)
        return value.reshape(shape)

    input_other = over_col(block_input)
    own_float = block_input.astype(F32)
    squares = plane_sum(jnp.sum(own_float * own_float, axis=1))
    inverse_natural = lax.rsqrt(squares / D + EPSILON)
    gains = lax.all_gather(jnp.stack([first_gain, second_gain]), ("row", "col"), axis=1, tiled=True)
    first_wide = lax.dynamic_slice_in_dim(gains[0], row * wide_width, wide_width, 0)
    second_wide = gains[1]

    rows_per_depth = wide_width // depths
    far = pick_columns(row, depth, 1, rows_per_depth, gate_weight, up_weight, (2, 3))
    far = [over_row(far[0], 2), over_row(far[1], 3)]
    gate_own, near = pick_columns(row, 0 * row, depths, rows_per_depth, gate_weight, up_weight, (0, 1))
    near = over_row(near, 1)
    far = lax.all_gather(jnp.stack(far), "dp", axis=0, tiled=False)
    gate_wide, up_wide = assemble(row, gate_own, near, far)

    def by_row(value):
        shape = value.shape
        value = value.reshape(shape[0], depths, ROWS, rows_per_depth)
        return value.transpose(0, 2, 1, 3).reshape(shape)

    input_wide = reorder(pair_cols(block_input, input_other))
    inverse_one = reorder(inverse_natural)[:, None]
    wide_one = (input_wide.astype(F32) * inverse_one * first_wide).astype(BF)
    input_blocks = input_wide.reshape(ROWS, COLS, part, wide_width)

    def to_token_shard(blocks):
        return [blocks[0]] + [over_row(blocks[k], k) for k in range(1, ROWS)]

    positions, documents = token_layout(segment_ids)
    positions = reorder(positions)
    documents = reorder(documents)
    key_index = reorder(jnp.arange(tokens, dtype=jnp.int32))
    cosine, sine = rotary_tables(positions, HD // 4)
    cosine = jnp.concatenate([cosine, cosine], axis=1)
    sine = jnp.concatenate([-sine, sine], axis=1)
    tables = (cosine[:span], sine[:span])
    layout = (documents[:span], key_index[:span], documents, key_index)

    def row_block(value, j):
        return value[j * span : (j + 1) * span]

    def pair_rows(value, a, b):
        return jnp.concatenate([row_block(value, a), row_block(value, b)], axis=0)

    def row_scatter(product, value):
        sent = over_row(product(pair_rows(value, 1, 3)).astype(BF), 1)
        kept = product(pair_rows(value, 0, 2)) + sent.astype(F32)
        return kept[:span], over_row(kept[span:].astype(BF), 2)

    def row_gather(value):
        near_block = over_row(value, 1)
        far_block = over_row(value, 2)
        return [value, near_block, far_block, over_row(far_block, 1)]

    kv_weight = jnp.concatenate([key_weight, value_weight], axis=1)
    kv_sent = over_row(matmul(pair_rows(wide_one, 1, 3), kv_weight).astype(BF), 1)
    query_kept, query_sent = row_scatter(lambda value: matmul(value, query_weight), wide_one)
    kv_kept = matmul(pair_rows(wide_one, 0, 2), kv_weight) + kv_sent.astype(F32)
    kv_other = over_row(kv_kept.astype(BF), 2)
    pair_cos, pair_sin = pair_rows(cosine, 0, 2), pair_rows(sine, 0, 2)
    kv_pair = turn_pair(kv_kept, kv_other, pair_cos, pair_sin, 1.0)

    def unpair(own, other):
        return jnp.concatenate([own[:span], other[:span], own[span:], other[span:]], axis=0)

    kv_all = unpair(kv_pair, over_row(kv_pair, 1))

    query, attended, logsum = attention_forward(query_kept, query_sent, tables, kv_all, layout)
    attended_blocks = row_gather(attended)

    def project(blocks):
        return matmul(jnp.concatenate(blocks, axis=0), output_weight).reshape(
            2, COLS, part, wide_width
        )

    near_out = project(attended_blocks[:2])
    far_out = project(attended_blocks[2:])
    out_sent = over_col(jnp.stack([near_out[:, 1], far_out[:, 1]]).astype(BF))
    out_sum = jnp.stack([near_out[:, 0], far_out[:, 0]]) + out_sent.astype(F32)
    out_sum = out_sum.reshape(ROWS, part, wide_width)
    out_rounded = out_sum.astype(BF)
    normed_two, inverse_two, own = norm_shard(
        row,
        to_token_shard([input_blocks[k, 0] for k in range(ROWS)]),
        to_token_shard([out_rounded[k] for k in range(ROWS)]),
        second_wide,
        depths,
    )
    half = part // 2
    at_x, at_y = over_row(own, 2), over_col(own)
    at_c = over_row(own, 1)
    at_xc, at_yc = over_row(at_x, 1), over_row(at_y, 1)
    at_xy = jnp.concatenate([over_row(at_y[:half], 2), over_col(at_x[half:])], axis=0)
    at_xyc = over_row(at_xy, 1)
    groups = ([own, at_c], [at_x, at_xc, at_y, at_yc], [at_xy, at_xyc])

    cot_wide = pair_cols(cotangent, over_col(after(cotangent, input_other)))
    down_blocks = [
        lax.dynamic_slice_in_dim(down_weight, (row ^ j) * ff, ff, 0) for j in range(ROWS)
    ]

    def hidden_part(j):
        return times_transposed(cot_wide, down_blocks[j])

    far_kept = (hidden_part(2) + over_row(hidden_part(3).astype(BF), 1).astype(F32)).astype(BF)
    near_kept = hidden_part(0) + over_row(hidden_part(1).astype(BF), 1).astype(F32)
    events = (kv_other, attended_blocks[2], attended_blocks[2], at_xy)
    far_received = [
        over_row(after(far_kept[k * span : (k + 1) * span], events[k]), 2) for k in range(ROWS)
    ]
    hidden_grad = near_kept + jnp.concatenate(far_received, axis=0).astype(F32)
    hidden_grad = reorder_col_major(hidden_grad)

    sizes = [len(g) * part for g in groups]
    offset = 0
    hiddens, gate_grads, up_grads, wides = [], [], [], []
    for group, size in zip(groups, sizes):
        wide = jnp.concatenate(group, axis=0)
        gate = matmul(wide, gate_wide)
        up = matmul(wide, up_wide)
        grad = hidden_grad[offset : offset + size]
        offset += size
        activation, gelu_back = jax.vjp(gelu_tanh, gate)
        hiddens.append((activation * up).astype(BF))
        gate_grads.append(gelu_back(grad * up)[0].astype(BF))
        up_grads.append((grad * activation).astype(BF))
        wides.append(wide)
    wide_two = jnp.concatenate(wides, axis=0)
    hidden = jnp.concatenate(hiddens, axis=0)
    gate_grad = jnp.concatenate(gate_grads, axis=0)
    up_grad = jnp.concatenate(up_grads, axis=0)

    def over_depth(value):
        return lax.psum_scatter(value, "dp", scatter_dimension=0, tiled=True)

    gate_grads = transposed_times(wide_two, gate_grad).astype(BF)
    up_grads = transposed_times(wide_two, up_grad).astype(BF)

    def feed_forward_grad(value):
        value = over_depth(value).reshape(ROWS, rows_per_depth, ff)
        blocks = exchange_rows([value[k] for k in range(ROWS)])
        blocks = [blocks[0]] + [over_row(blocks[k], k) for k in range(1, ROWS)]
        return jnp.concatenate(exchange_rows(blocks), axis=1).astype(F32)

    gate_weight_grad = feed_forward_grad(gate_grads)
    up_weight_grad = feed_forward_grad(up_grads)
    gate_grad, up_grad, _, _ = lax.optimization_barrier((gate_grad, up_grad, gate_grads, up_grads))

    def picks(value, blocks):
        return jnp.concatenate([value[b * part : (b + 1) * part] for b in blocks], axis=0)

    def plane_product(blocks):
        return times_transposed(picks(gate_grad, blocks), gate_wide) + times_transposed(
            picks(up_grad, blocks), up_wide
        )

    sent = over_row(plane_product((1, 3, 5, 7)).astype(BF), 1)
    kept = plane_product((0, 2, 4, 6)) + sent.astype(F32)
    kept = kept.reshape(2, 2, part, D)
    left, right = kept[..., : D // 2], kept[..., D // 2 :]
    left = left[0] + over_col(left[1].astype(BF)).astype(F32)
    left = left[0] + over_row(left[1].astype(BF), 2).astype(F32)
    right = right[:, 0] + over_row(right[:, 1].astype(BF), 2).astype(F32)
    right = right[0] + over_col(right[1].astype(BF)).astype(F32)
    wide_two_grad = by_row(jnp.concatenate([left, right], axis=1))

    cot_rel = reorder(cot_wide).reshape(ROWS, COLS, part, wide_width)
    cot_shard = to_token_shard([cot_rel[k, 0] for k in range(ROWS)])
    cot_shard = jnp.concatenate(exchange_rows(cot_shard), axis=1).astype(F32)
    scaled = wide_two_grad * second_wide
    inner = jnp.sum(scaled * normed_two, axis=1, keepdims=True)
    residual_grad = cot_shard + inverse_two * (scaled - normed_two * (inner / D))
    second_partial = jnp.sum(wide_two_grad * normed_two, axis=0)
    residual_back = residual_grad.astype(BF)

    residual_other = over_col(residual_back)
    residual_cols = jnp.concatenate([residual_back, residual_other], axis=0)
    column_blocks = exchange_rows(
        [residual_cols[:, k * wide_width : (k + 1) * wide_width] for k in range(ROWS)]
    )
    residual_blocks = [column_blocks[0]] + [over_row(column_blocks[k], k) for k in range(1, ROWS)]
    residual_wide = jnp.concatenate(residual_blocks, axis=0)

    grad_kept, grad_sent = row_scatter(
        lambda value: times_transposed(value, output_weight), residual_wide
    )
    query_grad, kv_grad = attention_backward(
        query, attended, grad_kept, grad_sent, logsum, tables, kv_all, layout
    )
    query_grad_all = jnp.concatenate(row_gather(query_grad), axis=0)
    kv_pair_grad = pair_rows(kv_grad, 0, 2) + over_row(pair_rows(kv_grad, 1, 3).astype(BF), 1).astype(
        F32
    )
    def flip_cols(value):
        shape = value.shape
        value = value.reshape(-1, COLS, part, shape[-1])
        return jnp.concatenate([value[:, 1:], value[:, :1]], axis=1).reshape(shape)

    kv_half = kv_pair_grad.astype(BF)
    kv_pair_grad = kv_half.astype(F32) + flip_cols(over_col(kv_half)).astype(F32)
    kv_half = kv_pair_grad.astype(BF)
    kv_back_pair = turn_pair(kv_half, over_row(kv_half, 2), pair_cos, pair_sin, -1.0)
    kv_back = unpair(kv_back_pair, over_row(kv_back_pair, 1))

    hidden_natural = jnp.concatenate(
        [
            lax.dynamic_slice_in_dim(hidden, ((col ^ y) * ROWS + (row ^ r)) * part, part, 0)
            for r in range(ROWS)
            for y in range(COLS)
        ],
        axis=0,
    )
    hidden_natural = after(hidden_natural, residual_back)
    hidden_blocks = row_gather(hidden_natural)
    down_partial = sum(matmul(h, w) for h, w in zip(hidden_blocks, down_blocks))
    down_grad = jnp.concatenate(
        exchange_rows([transposed_times(h, cot_wide).astype(BF) for h in hidden_blocks]), axis=0
    )
    down_grad = over_depth(down_grad).astype(F32)
    mlp = own_cols(down_partial) + over_col(other_cols(down_partial).astype(BF)).astype(F32)
    out_far = over_col(other_cols(out_sum))
    out_own = jnp.stack([own_cols(out_sum), out_far], axis=1).reshape(tokens, width)
    block_output = (own_float + reorder(out_own) + mlp).astype(BF)

    attended_all = jnp.concatenate(attended_blocks, axis=0)
    output_grad = transposed_times(attended_all, residual_wide).astype(BF)
    query_weight_grad = transposed_times(wide_one, query_grad_all).astype(BF)
    kv_weight_grad = transposed_times(wide_one, kv_back).astype(BF)
    pieces = query_width // wide_width
    shared = kv_weight_grad.shape[1]
    output_rows = output_grad.shape[0] // depths
    rest = jnp.concatenate(
        [output_grad.reshape(depths, output_rows, wide_width)]
        + [
            query_weight_grad[:, k * wide_width : (k + 1) * wide_width].reshape(
                depths, rows_per_depth, wide_width
            )
            for k in range(pieces)
        ]
        + [
            jnp.pad(kv_weight_grad, ((0, 0), (0, wide_width - shared))).reshape(
                depths, rows_per_depth, wide_width
            )
        ],
        axis=1,
    )
    rest = over_depth(rest.reshape(-1, wide_width)).astype(F32)
    output_grad = rest[:output_rows]
    query_weight_grad = jnp.concatenate(
        [
            rest[output_rows + k * rows_per_depth : output_rows + (k + 1) * rows_per_depth]
            for k in range(pieces)
        ],
        axis=1,
    )
    kv_weight_grad = rest[output_rows + pieces * rows_per_depth :, :shared]

    wide_one_partial = times_transposed(query_grad_all, query_weight)
    kv_rows = jnp.where(col == 0, kv_weight[:width], kv_weight[width:])
    wide_one_grad = (
        own_cols(wide_one_partial)
        + flip_cols(over_col(other_cols(wide_one_partial).astype(BF))).astype(F32)
        + times_transposed(kv_back, kv_rows)
    )
    normed_one = own_cols(input_wide).astype(F32) * inverse_one
    scaled = wide_one_grad * first_gain
    inner = plane_sum(reorder(jnp.sum(scaled * normed_one, axis=1)))
    inner = reorder(inner)[:, None]
    input_norm = inverse_one * (scaled - normed_one * (inner / D))
    first_partial = jnp.sum(wide_one_grad * normed_one, axis=0)
    input_grad = reorder(own_cols(residual_wide).astype(F32) + input_norm)

    second_partial = second_partial.reshape(ROWS, wide_width)
    second_partial = own_cols(second_partial) + over_col(other_cols(second_partial))
    blocks = exchange_rows([second_partial[k] for k in range(ROWS)])
    blocks = jnp.stack([blocks[0], blocks[2]]) + over_row(jnp.stack([blocks[1], blocks[3]]), 1)
    second_partial = blocks[0] + over_row(blocks[1], 2)
    gain_grads = jnp.stack([first_partial, second_partial])
    distance = 1
    while distance < depths:
        gain_grads = gain_grads + swap(gain_grads, "dp", distance)
        distance *= 2
    gain_width = width // depths
    gain_grads = lax.dynamic_slice_in_dim(gain_grads, depth * gain_width, gain_width, 1)

    return (
        block_output,
        input_grad,
        gain_grads[0],
        query_weight_grad,
        kv_weight_grad[:, :HD],
        kv_weight_grad[:, HD:],
        output_grad,
        gain_grads[1],
        gate_weight_grad,
        up_weight_grad,
        down_grad,
    )


def solution(mesh):
    return jax.shard_map(
        on_device,
        mesh=mesh,
        in_specs=(
            P("dp", ("row", "col")),
            P(("row", "col")),
            P("row", "col"),
            P("row", None),
            P("row", None),
            P("col", "row"),
            P(("row", "col")),
            P("row", "col"),
            P("row", "col"),
            P("col", "row"),
            P("dp", ("row", "col")),
            P("dp", None),
        ),
        out_specs=(
            P("dp", ("row", "col")),
            P("dp", ("row", "col")),
            P(("row", "col", "dp")),
            P(("row", "dp"), "col"),
            P(("row", "dp"), None),
            P(("row", "dp"), None),
            P(("col", "dp"), "row"),
            P(("row", "col", "dp")),
            P(("row", "dp"), "col"),
            P(("row", "dp"), "col"),
            P(("col", "dp"), "row"),
        ),
        check_vma=False,
    )
```

```python
import functools
import math

import jax
import jax.numpy as jnp
from jax import lax
from jax.experimental import pallas as pl
from jax.experimental.pallas import tpu as pltpu
from jax.sharding import PartitionSpec as P

D = 2560
HD = 256
DOCS = 6


EPSILON = 1e-06
NEGATIVE = -1e30

ROWS = 4
COLS = 2

BF = jnp.bfloat16
F32 = jnp.float32


def matmul(left, right):
    return jnp.dot(left, right, preferred_element_type=F32)


def times_transposed(left, right):
    return lax.dot_general(left, right, (((1,), (1,)), ((), ())), preferred_element_type=F32)


def transposed_times(left, right):
    return lax.dot_general(left, right, (((0,), (0,)), ((), ())), preferred_element_type=F32)


def gelu_tanh(value):
    return jax.nn.gelu(value, approximate=True)


def swap(value, axis, distance):
    size = lax.axis_size(axis)
    return lax.ppermute(value, axis, [(i, i ^ distance) for i in range(size)])


def over_row(value, distance):
    return swap(value, "row", distance)


def over_col(value):
    return swap(value, "col", 1)


def after(value, *others):
    return lax.optimization_barrier((value, *others))[0]


def rotary_tables(positions, quarter):
    freqs = jnp.exp(-jnp.log(10000.0) * jnp.arange(quarter, dtype=F32) / quarter)
    angles = positions.astype(F32)[:, None] * freqs[None, :]
    return (jnp.cos(angles), jnp.sin(angles))


def token_layout(segment_ids):
    count, length = segment_ids.shape
    index = jnp.arange(length, dtype=jnp.int32)[None, :]
    starts = jnp.concatenate(
        [
            jnp.ones((count, 1), jnp.int32),
            (segment_ids[:, 1:] != segment_ids[:, :-1]).astype(jnp.int32),
        ],
        axis=1,
    )
    first = lax.cummax(jnp.where(starts > 0, index, 0), axis=1)
    positions = (index - first).reshape(-1)
    documents = (segment_ids + DOCS * jnp.arange(count, dtype=jnp.int32)[:, None]).reshape(-1)
    return (positions, documents)


def turn(field, cosine, sine):
    first = field[:, : HD // 2]
    return jnp.concatenate(
        [first * cosine + pltpu.roll(first, HD // 4, 1) * sine, field[:, HD // 2 :]], axis=1
    )


def fill_bias(bias_ref, query_docs, query_index, key_docs, key_index):
    allowed = (query_docs[...] == key_docs[...]) & (key_index[...] <= query_index[...])
    bias_ref[...] = jnp.where(allowed, 0.0, NEGATIVE)


def forward_kernel(
    kept_ref, sent_ref, cos_ref, sin_ref, kv_ref, qd_ref, qi_ref, kd_ref, ki_ref,
    query_ref, attended_ref, logsum_ref, bias_ref,
):
    @pl.when(pl.program_id(0) == 0)
    def _():
        fill_bias(bias_ref, qd_ref, qi_ref, kd_ref, ki_ref)

    raw = kept_ref[...] + sent_ref[...].astype(F32)
    query = turn(raw, cos_ref[...], sin_ref[...]).astype(BF)
    query_ref[...] = query
    scores = times_transposed(query, kv_ref[:, :HD]) * (1.0 / math.sqrt(HD)) + bias_ref[...]
    peak = jnp.max(scores, axis=1, keepdims=True)
    weights = jnp.exp(scores - peak)
    total = jnp.sum(weights, axis=1, keepdims=True)
    logsum_ref[0] = peak + jnp.log(total)
    probs = (weights * (1.0 / total)).astype(BF)
    attended_ref[...] = matmul(probs, kv_ref[:, HD:]).astype(BF)


def attention_forward(kept, sent, tables, kv, layout):
    span, width = sent.shape
    length = kv.shape[0]
    heads = width // HD
    query_docs, query_index, key_docs, key_index = layout
    whole = lambda a: pl.BlockSpec(a.shape, lambda h: (0, 0))
    small = [
        tables[0], tables[1], kv, query_docs[:, None], query_index[:, None], key_docs[None], key_index[None]
    ]
    head = pl.BlockSpec((span, HD), lambda h: (0, h))
    return pl.pallas_call(
        forward_kernel,
        grid=(heads,),
        in_specs=[head, head] + [whole(a) for a in small],
        out_specs=[head, head, pl.BlockSpec((1, span, 1), lambda h: (h, 0, 0))],
        out_shape=[
            jax.ShapeDtypeStruct((span, width), BF),
            jax.ShapeDtypeStruct((span, width), BF),
            jax.ShapeDtypeStruct((heads, span, 1), F32),
        ],
        scratch_shapes=[pltpu.VMEM((span, length), F32)],
        name="attention_forward",
    )(kept, sent, *small)


def backward_kernel(
    query_ref, attended_ref, kept_ref, sent_ref, logsum_ref, cos_ref, sin_ref, kv_ref, qd_ref, qi_ref,
    kd_ref, ki_ref, query_grad_ref, kv_grad_ref, bias_ref,
):
    @pl.when(pl.program_id(0) == 0)
    def _():
        fill_bias(bias_ref, qd_ref, qi_ref, kd_ref, ki_ref)
        kv_grad_ref[...] = jnp.zeros_like(kv_grad_ref)

    scale = 1.0 / math.sqrt(HD)
    query = query_ref[...]
    grad = (kept_ref[...] + sent_ref[...].astype(F32)).astype(BF)
    keys, values = kv_ref[:, :HD], kv_ref[:, HD:]
    scores = times_transposed(query, keys) * scale + bias_ref[...]
    weights = jnp.exp(scores - logsum_ref[0])
    kv_grad_ref[:, HD:] += transposed_times(weights.astype(BF), grad)
    delta = jnp.sum(grad.astype(F32) * attended_ref[...].astype(F32), axis=1, keepdims=True)
    score_grad = (weights * (times_transposed(grad, values) - delta)).astype(BF)
    query_grad = turn(matmul(score_grad, keys) * scale, cos_ref[...], -sin_ref[...])
    query_grad_ref[...] = query_grad.astype(BF)
    kv_grad_ref[:, :HD] += transposed_times(score_grad, query) * scale


def attention_backward(query, attended, kept, sent, logsum, tables, kv, layout):
    span, width = sent.shape
    length = kv.shape[0]
    heads = width // HD
    query_docs, query_index, key_docs, key_index = layout
    whole = lambda a: pl.BlockSpec(a.shape, lambda h: (0, 0))
    small = [
        tables[0], tables[1], kv, query_docs[:, None], query_index[:, None], key_docs[None], key_index[None]
    ]
    head = pl.BlockSpec((span, HD), lambda h: (0, h))
    return pl.pallas_call(
        backward_kernel,
        grid=(heads,),
        in_specs=[head, head, head, head, pl.BlockSpec((1, span, 1), lambda h: (h, 0, 0))]
        + [whole(a) for a in small],
        out_specs=[head, pl.BlockSpec((length, 2 * HD), lambda h: (0, 0))],
        out_shape=[
            jax.ShapeDtypeStruct((span, width), BF),
            jax.ShapeDtypeStruct((length, 2 * HD), F32),
        ],
        scratch_shapes=[pltpu.VMEM((span, length), F32)],
        name="attention_backward",
    )(query, attended, kept, sent, logsum, *small)


def turn_kernel(kept_ref, other_ref, cos_ref, sin_ref, out_ref, *, sign):
    span = kept_ref.shape[0] // 2
    other = jnp.concatenate([other_ref[span:], other_ref[:span]], axis=0)
    total = kept_ref[...].astype(F32) + other.astype(F32)
    keys = turn(total[:, :HD], cos_ref[...], sin_ref[...] * sign)
    out_ref[...] = jnp.concatenate([keys, total[:, HD:]], axis=1).astype(BF)


def turn_pair(kept, other, cosine, sine, sign):
    return pl.pallas_call(
        functools.partial(turn_kernel, sign=sign),
        out_shape=jax.ShapeDtypeStruct(kept.shape, BF),
        name="turn_pair",
    )(kept, other, cosine, sine)


def norm_kernel(row_ref, *refs, depths):
    input_refs, out_refs = refs[:ROWS], refs[ROWS : 2 * ROWS]
    gain_ref, normed_ref, inverse_ref, wide_ref = refs[2 * ROWS :]
    row = row_ref[0]
    block = D // ROWS
    for j in range(ROWS):
        at = pl.ds(pl.multiple_of((row ^ j) * block, 128), block)
        normed_ref[:, at] = input_refs[j][...].astype(F32) + out_refs[j][...].astype(F32)
    residual = normed_ref[...]
    inverse = lax.rsqrt(jnp.sum(residual * residual, axis=1, keepdims=True) / D + EPSILON)
    normed = residual * inverse
    normed_ref[...] = normed
    inverse_ref[...] = inverse
    wide = normed * gain_ref[...]
    chunk = block // depths
    pieces = [
        wide[:, r * block + z * chunk : r * block + (z + 1) * chunk]
        for z in range(depths)
        for r in range(ROWS)
    ]
    wide_ref[...] = jnp.concatenate(pieces, axis=1).astype(BF)


def norm_back_kernel(row_ref, *refs, depths):
    left_ref, left_other_ref, right_ref, right_other_ref, normed_ref, inverse_ref, gain_ref = refs[:7]
    cot_refs = refs[7 : 7 + ROWS]
    back_ref, gain_grad_ref, grad_ref = refs[7 + ROWS :]
    row = row_ref[0]
    block = D // ROWS
    chunk = block // depths
    grad = jnp.concatenate(
        [
            left_ref[...] + left_other_ref[...].astype(F32),
            right_ref[...] + right_other_ref[...].astype(F32),
        ],
        axis=1,
    )
    grad = jnp.concatenate(
        [
            grad[:, (z * ROWS + r) * chunk : (z * ROWS + r + 1) * chunk]
            for r in range(ROWS)
            for z in range(depths)
        ],
        axis=1,
    )
    normed = normed_ref[...]
    gain_grad_ref[...] = jnp.sum(grad * normed, axis=0, keepdims=True)
    scaled = grad * gain_ref[...]
    inner = jnp.sum(scaled * normed, axis=1, keepdims=True)
    grad_ref[...] = inverse_ref[...] * (scaled - normed * (inner / D))
    for j in range(ROWS):
        at = pl.ds(pl.multiple_of((row ^ j) * block, 128), block)
        back_ref[j] = (cot_refs[j][...].astype(F32) + grad_ref[:, at]).astype(BF)


def norm_back(row, sums, normed, inverse, gain, cots, depths):
    part = normed.shape[0]
    vmem = pl.BlockSpec(memory_space=pltpu.VMEM)
    return pl.pallas_call(
        functools.partial(norm_back_kernel, depths=depths),
        in_specs=[pl.BlockSpec(memory_space=pltpu.SMEM)] + [vmem] * (7 + ROWS),
        out_specs=[vmem] * 2,
        out_shape=[
            jax.ShapeDtypeStruct((ROWS, part, D // ROWS), BF),
            jax.ShapeDtypeStruct((1, D), F32),
        ],
        scratch_shapes=[pltpu.VMEM((part, D), F32)],
        name="norm_back",
    )(row.reshape(1), *sums, normed, inverse, gain[None], *cots)


def norm_shard(row, inputs, outs, gain, depths):
    part = inputs[0].shape[0]
    vmem = pl.BlockSpec(memory_space=pltpu.VMEM)
    return pl.pallas_call(
        functools.partial(norm_kernel, depths=depths),
        in_specs=[pl.BlockSpec(memory_space=pltpu.SMEM)] + [vmem] * (2 * ROWS + 1),
        out_specs=[vmem] * 3,
        out_shape=[
            jax.ShapeDtypeStruct((part, D), F32),
            jax.ShapeDtypeStruct((part, 1), F32),
            jax.ShapeDtypeStruct((part, D), BF),
        ],
        name="norm_shard",
    )(row.reshape(1), *inputs, *outs, gain[None])


def pick_kernel(where_ref, gate_ref, up_ref, *out_refs, blocks):
    width = gate_ref.shape[1] // ROWS
    for row in range(ROWS):

        @pl.when(where_ref[0] == row)
        def _(row=row):
            for block, out_ref in zip(blocks, out_refs):
                at = (row ^ block) * width
                out_ref[:, :width] = gate_ref[:, at : at + width]
                out_ref[:, width:] = up_ref[:, at : at + width]


def pick_columns(row, first, count, rows, gate, up, blocks):
    width = gate.shape[1] // ROWS
    source = pl.BlockSpec((rows, gate.shape[1]), lambda i, where: (where[1] + i, 0))
    return pl.pallas_call(
        functools.partial(pick_kernel, blocks=blocks),
        grid_spec=pltpu.PrefetchScalarGridSpec(
            num_scalar_prefetch=1,
            grid=(count,),
            in_specs=[source, source],
            out_specs=[pl.BlockSpec((rows, 2 * width), lambda i, where: (i, 0))] * len(blocks),
        ),
        out_shape=[jax.ShapeDtypeStruct((count * rows, 2 * width), BF)] * len(blocks),
        name="pick_columns",
    )(jnp.stack([row, first]), gate, up)


def assemble_kernel(row_ref, *refs):
    sources, (gate_ref, up_ref) = refs[:ROWS], refs[ROWS:]
    width = gate_ref.shape[1]
    mine = pl.program_id(0) ^ row_ref[0]
    for j in range(ROWS):

        @pl.when(mine == j)
        def _(j=j):
            gate_ref[...] = sources[j][:, :width]
            up_ref[...] = sources[j][:, width:]


def assemble(row, sources, depths):
    rows, width = sources[0].shape[0] // depths, sources[0].shape[1] // 2

    def source(j):
        return pl.BlockSpec(
            (rows, 2 * width), lambda r, z, row: (jnp.where((r ^ row[0]) == j, z, 0), 0)
        )

    shape = jax.ShapeDtypeStruct((depths * ROWS * rows, width), BF)
    return pl.pallas_call(
        assemble_kernel,
        grid_spec=pltpu.PrefetchScalarGridSpec(
            num_scalar_prefetch=1,
            grid=(ROWS, depths),
            in_specs=[source(j) for j in range(ROWS)],
            out_specs=[pl.BlockSpec((rows, width), lambda r, z, row: (z * ROWS + r, 0))] * 2,
        ),
        out_shape=[shape, shape],
        name="assemble",
    )(row.reshape(1), *sources)


def finish_kernel(row_ref, *refs):
    sources, (gate_ref, up_ref) = refs[:ROWS], refs[ROWS:]
    width = gate_ref.shape[1] // ROWS
    for row in range(ROWS):

        @pl.when(row_ref[0] == row)
        def _(row=row):
            for j, source in enumerate(sources):
                at = (row ^ j) * width
                gate_ref[:, at : at + width] = source[:, :width].astype(F32)
                up_ref[:, at : at + width] = source[:, width:].astype(F32)


def finish(row, sources):
    rows, width = sources[0].shape[0], sources[0].shape[1] // 2
    vmem = pl.BlockSpec(memory_space=pltpu.VMEM)
    shape = jax.ShapeDtypeStruct((rows, ROWS * width), F32)
    return pl.pallas_call(
        finish_kernel,
        in_specs=[pl.BlockSpec(memory_space=pltpu.SMEM)] + [vmem] * ROWS,
        out_specs=[vmem] * 2,
        out_shape=[shape, shape],
        name="finish",
    )(row.reshape(1), *sources)


def reorder_kernel(order_ref, source_ref, out_ref):
    out_ref[...] = source_ref[...]


def reorder_blocks(order, value):
    count, (length, width) = order.shape[0], value.shape
    return pl.pallas_call(
        reorder_kernel,
        grid_spec=pltpu.PrefetchScalarGridSpec(
            num_scalar_prefetch=1,
            grid=(count,),
            in_specs=[pl.BlockSpec((length // count, width), lambda i, order: (order[i], 0))],
            out_specs=pl.BlockSpec((length // count, width), lambda i, order: (i, 0)),
        ),
        out_shape=jax.ShapeDtypeStruct(value.shape, value.dtype),
        name="reorder",
    )(order, value)


def open_kernel(where_ref, own_ref, other_ref, inverse_ref, gain_ref, input_ref, wide_ref):
    width = own_ref.shape[1]
    own, other = own_ref[...].astype(F32), other_ref[...].astype(F32)
    for col in range(COLS):

        @pl.when(where_ref[0] == col)
        def _(col=col):
            both = jnp.concatenate([own, other] if col == 0 else [other, own], axis=1)
            input_ref[...] = both.astype(BF)
            wide_ref[...] = (both * inverse_ref[...] * gain_ref[...]).astype(BF)


def open_block(col, order, own, other, inverse, gain):
    count, (length, width) = order.shape[0], own.shape
    rows = length // count
    source = pl.BlockSpec((rows, width), lambda i, where: (where[1 + i], 0))
    out = pl.BlockSpec((rows, COLS * width), lambda i, where: (i, 0))
    shape = jax.ShapeDtypeStruct((length, COLS * width), BF)
    return pl.pallas_call(
        open_kernel,
        grid_spec=pltpu.PrefetchScalarGridSpec(
            num_scalar_prefetch=1,
            grid=(count,),
            in_specs=[
                source,
                source,
                pl.BlockSpec((rows, 1), lambda i, where: (where[1 + i], 0)),
                pl.BlockSpec((1, COLS * width), lambda i, where: (0, 0)),
            ],
            out_specs=[out, out],
        ),
        out_shape=[shape, shape],
        name="open_block",
    )(jnp.concatenate([col.reshape(1), order]), own, other, inverse, gain[None])


def down_grad_kernel(row_ref, *refs):
    sources, (cot_ref, out_ref) = refs[:ROWS], refs[ROWS:]
    for j in range(ROWS):

        @pl.when((pl.program_id(0) ^ row_ref[0]) == j)
        def _(j=j):
            out_ref[...] = transposed_times(sources[j][...], cot_ref[...]).astype(BF)


def down_gradient(row, hiddens, cot):
    ff, width = hiddens[0].shape[1], cot.shape[1]
    whole = lambda a: pl.BlockSpec(a.shape, lambda r, row: (0, 0))
    return pl.pallas_call(
        down_grad_kernel,
        grid_spec=pltpu.PrefetchScalarGridSpec(
            num_scalar_prefetch=1,
            grid=(ROWS,),
            in_specs=[whole(a) for a in (*hiddens, cot)],
            out_specs=pl.BlockSpec((ff, width), lambda r, row: (r, 0)),
        ),
        out_shape=jax.ShapeDtypeStruct((ROWS * ff, width), BF),
        name="down_gradient",
    )(row.reshape(1), *hiddens, cot)


def on_device(
    block_input,
    first_gain,
    query_weight,
    key_weight,
    value_weight,
    output_weight,
    second_gain,
    gate_weight,
    up_weight,
    down_weight,
    cotangent,
    segment_ids,
):
    row = lax.axis_index("row")
    col = lax.axis_index("col")
    depth = lax.axis_index("dp")
    depths = lax.axis_size("dp")
    assert lax.axis_size("row") == ROWS and lax.axis_size("col") == COLS
    tokens, width = block_input.shape
    wide_width = COLS * width
    span = tokens // ROWS
    part = span // COLS
    query_width = query_weight.shape[1]
    heads = query_width // HD
    ff_width = gate_weight.shape[1]
    ff = ff_width // ROWS

    def exchange_rows(blocks):
        low, high = (row & 1) == 1, (row >> 1) == 1
        picked = [
            jnp.where(
                high,
                jnp.where(low, blocks[j ^ 3], blocks[j ^ 2]),
                jnp.where(low, blocks[j ^ 1], blocks[j]),
            )
            for j in range(ROWS)
        ]
        return picked

    blocks = jnp.arange(ROWS * COLS, dtype=jnp.int32)
    row_major = ((row ^ (blocks // COLS)) * COLS + (col ^ (blocks % COLS))).astype(jnp.int32)
    col_major = ((row ^ (blocks % ROWS)) * COLS + (col ^ (blocks // ROWS))).astype(jnp.int32)
    from_col_major = ((col ^ (blocks % COLS)) * ROWS + (row ^ (blocks // COLS))).astype(jnp.int32)

    def reorder(value):
        if value.ndim == 2:
            return reorder_blocks(row_major, value)
        value = value.reshape(1, ROWS * COLS, part)
        chosen = row_major[:, None, None] == blocks[None, :, None]
        return jnp.sum(jnp.where(chosen, value, 0), axis=1, dtype=value.dtype).reshape(tokens)

    def pair_cols(own, other):
        return jnp.concatenate([jnp.where(col == 0, own, other), jnp.where(col == 0, other, own)], axis=1)

    def own_cols(value):
        return jnp.where(col == 0, value[..., :width], value[..., width:])

    def other_cols(value):
        return jnp.where(col == 0, value[..., width:], value[..., :width])

    def plane_sum(value):
        value = value.reshape(ROWS * COLS, part)
        value = value + over_row(value, 1)
        value = value + over_row(value, 2)
        return (value + over_col(value)).reshape(tokens), value

    input_other = over_col(block_input)
    own_float = block_input.astype(F32)
    squares, row_squares = plane_sum(jnp.sum(own_float * own_float, axis=1))
    inverse_natural = lax.rsqrt(squares / D + EPSILON)
    gains = jnp.stack([first_gain, second_gain])
    gains = pair_cols(gains, over_col(gains))
    first_wide = gains[0]
    second_wide = [gains[1]] + [over_row(gains[1], k) for k in range(1, ROWS)]
    second_wide = jnp.concatenate(exchange_rows(second_wide))

    rows_per_depth = wide_width // depths
    far = pick_columns(row, depth, 1, rows_per_depth, gate_weight, up_weight, (2, 3))
    far = [after(far[0], second_wide, row_squares), after(far[1], second_wide, row_squares)]
    far = [over_row(far[0], 2), over_row(far[1], 3)]
    gate_own, near = pick_columns(row, 0 * row, depths, rows_per_depth, gate_weight, up_weight, (0, 1))
    near = over_row(near, 1)
    input_wide, wide_one = open_block(
        col, row_major, block_input, input_other, inverse_natural[:, None], first_wide
    )
    inverse_one = reorder(inverse_natural)[:, None]
    input_blocks = input_wide.reshape(ROWS, COLS, part, wide_width)

    def to_token_shard(blocks):
        return [blocks[0]] + [over_row(blocks[k], k) for k in range(1, ROWS)]

    positions, documents = token_layout(segment_ids)
    positions = reorder(positions)
    documents = reorder(documents)
    key_index = reorder(jnp.arange(tokens, dtype=jnp.int32))
    cosine, sine = rotary_tables(positions, HD // 4)
    cosine = jnp.concatenate([cosine, cosine], axis=1)
    sine = jnp.concatenate([-sine, sine], axis=1)
    tables = (cosine[:span], sine[:span])
    layout = (documents[:span], key_index[:span], documents, key_index)

    def row_block(value, j):
        return value[j * span : (j + 1) * span]

    def pair_rows(value, a, b):
        return jnp.concatenate([row_block(value, a), row_block(value, b)], axis=0)

    def row_scatter(product, value):
        sent = over_row(product(pair_rows(value, 1, 3)).astype(BF), 1)
        kept = product(pair_rows(value, 0, 2)) + sent.astype(F32)
        return kept[:span], over_row(kept[span:].astype(BF), 2)

    def row_gather(value):
        near_block = over_row(value, 1)
        far_block = over_row(value, 2)
        return [value, near_block, far_block, over_row(far_block, 1)]

    kv_weight = jnp.concatenate([key_weight, value_weight], axis=1)
    kv_sent = over_row(matmul(pair_rows(wide_one, 1, 3), kv_weight).astype(BF), 1)
    query_kept, query_sent = row_scatter(lambda value: matmul(value, query_weight), wide_one)
    far = [after(far[0], wide_one), after(far[1], query_kept)]
    far = [lax.all_gather(piece, "dp", axis=0, tiled=True) for piece in far]
    gate_wide, up_wide = assemble(row, [gate_own, near, *far], depths)
    kv_kept = matmul(pair_rows(wide_one, 0, 2), kv_weight) + kv_sent.astype(F32)
    kv_other = over_row(kv_kept.astype(BF), 2)
    pair_cos, pair_sin = pair_rows(cosine, 0, 2), pair_rows(sine, 0, 2)
    kv_pair = turn_pair(kv_kept, kv_other, pair_cos, pair_sin, 1.0)

    def unpair(own, other):
        return jnp.concatenate([own[:span], other[:span], own[span:], other[span:]], axis=0)

    kv_all = unpair(kv_pair, over_row(kv_pair, 1))

    query, attended, logsum = attention_forward(query_kept, query_sent, tables, kv_all, layout)
    attended_blocks = row_gather(attended)

    def project(blocks):
        return matmul(jnp.concatenate(blocks, axis=0), output_weight).reshape(
            2, COLS, part, wide_width
        )

    near_out = project(attended_blocks[:2])
    far_out = project(attended_blocks[2:])
    out_sent = over_col(jnp.stack([near_out[:, 1], far_out[:, 1]]).astype(BF))
    out_sum = jnp.stack([near_out[:, 0], far_out[:, 0]]) + out_sent.astype(F32)
    out_sum = out_sum.reshape(ROWS, part, wide_width)
    out_rounded = out_sum.astype(BF)
    normed_two, inverse_two, own = norm_shard(
        row,
        to_token_shard([input_blocks[k, 0] for k in range(ROWS)]),
        to_token_shard([out_rounded[k] for k in range(ROWS)]),
        second_wide,
        depths,
    )
    half = part // 2
    at_x, at_y = over_row(own, 2), over_col(own)
    at_c = over_row(own, 1)
    at_xc, at_yc = over_row(at_x, 1), over_row(at_y, 1)
    at_xy = jnp.concatenate([over_row(at_y[:half], 2), over_col(at_x[half:])], axis=0)
    at_xyc = over_row(at_xy, 1)
    groups = ([own, at_c], [at_x, at_xc, at_y, at_yc], [at_xy, at_xyc])

    cot_wide = pair_cols(cotangent, over_col(after(cotangent, input_other)))
    down_blocks = [
        lax.dynamic_slice_in_dim(down_weight, (row ^ j) * ff, ff, 0) for j in range(ROWS)
    ]

    def hidden_part(j):
        return times_transposed(cot_wide, down_blocks[j])

    far_kept = (hidden_part(2) + over_row(hidden_part(3).astype(BF), 1).astype(F32)).astype(BF)
    near_kept = hidden_part(0) + over_row(hidden_part(1).astype(BF), 1).astype(F32)
    events = (kv_other, attended_blocks[2], attended_blocks[2], at_xy)
    far_received = [
        over_row(after(far_kept[k * span : (k + 1) * span], events[k]), 2) for k in range(ROWS)
    ]
    hidden_grad = near_kept + jnp.concatenate(far_received, axis=0).astype(F32)
    hidden_grad = reorder_blocks(col_major, hidden_grad)

    sizes = [len(g) * part for g in groups]
    offset = 0
    hiddens, gate_grads, up_grads, wides = [], [], [], []
    for group, size in zip(groups, sizes):
        wide = jnp.concatenate(group, axis=0)
        gate = matmul(wide, gate_wide)
        up = matmul(wide, up_wide)
        grad = hidden_grad[offset : offset + size]
        offset += size
        activation, gelu_back = jax.vjp(gelu_tanh, gate)
        hiddens.append((activation * up).astype(BF))
        gate_grads.append(gelu_back(grad * up)[0].astype(BF))
        up_grads.append((grad * activation).astype(BF))
        wides.append(wide)
    wide_two = jnp.concatenate(wides, axis=0)
    hidden = jnp.concatenate(hiddens, axis=0)
    both_grads = jnp.concatenate(
        [jnp.concatenate([a, b], axis=1) for a, b in zip(gate_grads, up_grads)], axis=0
    )
    gate_grad = jnp.concatenate(gate_grads, axis=0)
    up_grad = jnp.concatenate(up_grads, axis=0)

    def over_depth(value):
        return lax.psum_scatter(value, "dp", scatter_dimension=0, tiled=True)

    feed = transposed_times(wide_two, both_grads).astype(BF)
    gate_grad, up_grad, _ = lax.optimization_barrier((gate_grad, up_grad, feed))
    feed = over_depth(feed)

    def feed_block(k):
        return lax.dynamic_slice_in_dim(feed, (row ^ k) * rows_per_depth, rows_per_depth, 0)

    feed = [feed_block(0)] + [over_row(feed_block(k), k) for k in range(1, ROWS)]
    gate_weight_grad, up_weight_grad = finish(row, feed)

    def picks(value, blocks):
        return jnp.concatenate([value[b * part : (b + 1) * part] for b in blocks], axis=0)

    def plane_product(blocks):
        return times_transposed(picks(gate_grad, blocks), gate_wide) + times_transposed(
            picks(up_grad, blocks), up_wide
        )

    sent = over_row(plane_product((1, 5, 7, 3)).astype(BF), 1)
    kept = plane_product((0, 4, 6, 2)) + sent.astype(F32)
    middle = D // 2
    left_near = over_col(kept[part : 3 * part, :middle].astype(BF))
    right_near = over_row(kept[2 * part :, middle:].astype(BF), 2)
    left_far = over_row((kept[3 * part :, :middle] + left_near[part:].astype(F32)).astype(BF), 2)
    right_far = over_col(
        (kept[part : 2 * part, middle:] + right_near[:part].astype(F32)).astype(BF)
    )
    left = kept[:part, :middle] + left_near[:part].astype(F32)
    right = kept[:part, middle:] + right_near[part:].astype(F32)

    cot_rel = reorder(cot_wide).reshape(ROWS, COLS, part, wide_width)
    cot_shard = to_token_shard([cot_rel[k, 0] for k in range(ROWS)])
    residual_back, second_partial = norm_back(
        row, (left, left_far, right, right_far), normed_two, inverse_two, second_wide, cot_shard, depths
    )

    residual_other = over_col(residual_back)
    column_blocks = [
        jnp.concatenate([residual_back[k], residual_other[k]], axis=0) for k in range(ROWS)
    ]
    residual_blocks = [column_blocks[0]] + [over_row(column_blocks[k], k) for k in range(1, ROWS)]
    residual_wide = jnp.concatenate(residual_blocks, axis=0)

    grad_kept, grad_sent = row_scatter(
        lambda value: times_transposed(value, output_weight), residual_wide
    )
    query_grad, kv_grad = attention_backward(
        query, attended, grad_kept, grad_sent, logsum, tables, kv_all, layout
    )
    query_grad_all = jnp.concatenate(row_gather(query_grad), axis=0)
    kv_pair_grad = pair_rows(kv_grad, 0, 2) + over_row(pair_rows(kv_grad, 1, 3).astype(BF), 1).astype(
        F32
    )
    def flip_cols(value):
        shape = value.shape
        value = value.reshape(-1, COLS, part, shape[-1])
        return jnp.concatenate([value[:, 1:], value[:, :1]], axis=1).reshape(shape)

    kv_half = kv_pair_grad.astype(BF)
    kv_pair_grad = kv_half.astype(F32) + flip_cols(over_col(kv_half)).astype(F32)
    kv_half = kv_pair_grad.astype(BF)
    kv_back_pair = turn_pair(kv_half, over_row(kv_half, 2), pair_cos, pair_sin, -1.0)
    kv_back = unpair(kv_back_pair, over_row(kv_back_pair, 1))

    hidden_natural = reorder_blocks(from_col_major, hidden)
    hidden_natural = after(hidden_natural, residual_back)
    hidden_blocks = row_gather(hidden_natural)
    down_partial = sum(matmul(h, w) for h, w in zip(hidden_blocks, down_blocks))
    down_grad = down_gradient(row, hidden_blocks, cot_wide)
    mlp = own_cols(down_partial) + over_col(other_cols(down_partial).astype(BF)).astype(F32)
    out_far = over_col(other_cols(out_sum))
    out_own = jnp.stack([own_cols(out_sum), out_far], axis=1).reshape(tokens, width)
    block_output = (own_float + reorder(out_own) + mlp).astype(BF)

    attended_all = jnp.concatenate(attended_blocks, axis=0)
    output_grad = transposed_times(attended_all, residual_wide).astype(BF)
    query_weight_grad = transposed_times(wide_one, query_grad_all).astype(BF)
    kv_weight_grad = transposed_times(wide_one, kv_back).astype(BF)
    pieces = query_width // wide_width
    shared = kv_weight_grad.shape[1]
    output_rows = output_grad.shape[0] // depths
    down_rows = down_grad.shape[0] // depths
    rest = jnp.concatenate(
        [down_grad.reshape(depths, down_rows, wide_width), output_grad.reshape(depths, output_rows, wide_width)]
        + [
            query_weight_grad[:, k * wide_width : (k + 1) * wide_width].reshape(
                depths, rows_per_depth, wide_width
            )
            for k in range(pieces)
        ]
        + [
            jnp.pad(kv_weight_grad, ((0, 0), (0, wide_width - shared))).reshape(
                depths, rows_per_depth, wide_width
            )
        ],
        axis=1,
    )
    rest = over_depth(rest.reshape(-1, wide_width)).astype(F32)
    down_grad, rest = rest[:down_rows], rest[down_rows:]
    output_grad = rest[:output_rows]
    query_weight_grad = jnp.concatenate(
        [
            rest[output_rows + k * rows_per_depth : output_rows + (k + 1) * rows_per_depth]
            for k in range(pieces)
        ],
        axis=1,
    )
    kv_weight_grad = rest[output_rows + pieces * rows_per_depth :, :shared]

    wide_one_partial = times_transposed(query_grad_all, query_weight)
    kv_rows = jnp.where(col == 0, kv_weight[:width], kv_weight[width:])
    wide_one_grad = (
        own_cols(wide_one_partial)
        + flip_cols(over_col(other_cols(wide_one_partial).astype(BF))).astype(F32)
        + times_transposed(kv_back, kv_rows)
    )
    normed_one = own_cols(input_wide).astype(F32) * inverse_one
    scaled = wide_one_grad * first_gain
    inner, _ = plane_sum(reorder(jnp.sum(scaled * normed_one, axis=1)))
    inner = reorder(inner)[:, None]
    input_norm = inverse_one * (scaled - normed_one * (inner / D))
    first_partial = jnp.sum(wide_one_grad * normed_one, axis=0)
    input_grad = reorder(own_cols(residual_wide).astype(F32) + input_norm)

    second_partial = second_partial.reshape(ROWS, wide_width)
    second_partial = own_cols(second_partial) + over_col(other_cols(second_partial))
    blocks = exchange_rows([second_partial[k] for k in range(ROWS)])
    blocks = jnp.stack([blocks[0], blocks[2]]) + over_row(jnp.stack([blocks[1], blocks[3]]), 1)
    second_partial = blocks[0] + over_row(blocks[1], 2)
    gain_grads = jnp.stack([first_partial, second_partial])
    distance = 1
    while distance < depths:
        gain_grads = gain_grads + swap(gain_grads, "dp", distance)
        distance *= 2
    gain_width = width // depths
    gain_grads = lax.dynamic_slice_in_dim(gain_grads, depth * gain_width, gain_width, 1)

    return (
        block_output,
        input_grad,
        gain_grads[0],
        query_weight_grad,
        kv_weight_grad[:, :HD],
        kv_weight_grad[:, HD:],
        output_grad,
        gain_grads[1],
        gate_weight_grad,
        up_weight_grad,
        down_grad,
    )


def solution(mesh):
    return jax.shard_map(
        on_device,
        mesh=mesh,
        in_specs=(
            P("dp", ("row", "col")),
            P(("row", "col")),
            P("row", "col"),
            P("row", None),
            P("row", None),
            P("col", "row"),
            P(("row", "col")),
            P("row", "col"),
            P("row", "col"),
            P("col", "row"),
            P("dp", ("row", "col")),
            P("dp", None),
        ),
        out_specs=(
            P("dp", ("row", "col")),
            P("dp", ("row", "col")),
            P(("row", "col", "dp")),
            P(("row", "dp"), "col"),
            P(("row", "dp"), None),
            P(("row", "dp"), None),
            P(("col", "dp"), "row"),
            P(("row", "col", "dp")),
            P(("row", "dp"), "col"),
            P(("row", "dp"), "col"),
            P(("col", "dp"), "row"),
        ),
        check_vma=False,
    )
```
